32 devices in a mesh: ens: 4 (over y, x), tile: 8 (over z, core).
Axes of the slice: x: 2, y: 2, z: 4, core: 2. Of those that a mesh axis runs over, the one named last changes fastest.
Arguments:
- air_latent_array: bfloat16 [4, 8, 16, 384], P('ens', 'tile'), may hold values from -6 to 6
- air_exchange_projection: bfloat16 [384, 128], replicated, may hold values from -0.3125 to 0.3125
- marine_latent_array: bfloat16 [4, 32, 64, 256], P('ens', None, 'tile'), may hold values from -6 to 6
- driver_projection_matrix: bfloat16 [128, 256], replicated, may hold values from -0.5 to 0.5
- spatial_kernel_taps: float32 [9, 256], replicated, may hold values from -1.5 to 1.5
- layernorm_multiplier: float32 [256], replicated, may hold values from 0.25 to 1.75
- pointwise_widen_matrix: bfloat16 [256, 1024], replicated, may hold values from -0.375 to 0.375
- pointwise_shrink_matrix: bfloat16 [1024, 256], replicated, may hold values from -0.1875 to 0.1875
- thermal_projection_matrix: bfloat16 [256, 128], replicated, may hold values from -0.375 to 0.375
- intersecting_air_sites: int32 [4, 32, 64], P(None, None, 'tile'), may hold values from 0 to 15, as said below
- margin_multiplier: int32 [4, 32, 64], P(None, None, 'tile'), may hold values from 1 to 8
- terrain_water_indicator: int32 [32, 64], P(None, 'tile'), may hold values from 0 to 1, as said below
- marine_successor_adjoint: bfloat16 [4, 32, 64, 256], P('ens', None, 'tile'), may hold values from -6 to 6
Outputs:
- marine_successor_latent: bfloat16 [4, 32, 64, 256], P('ens', None, 'tile')
- sst_atm: bfloat16 [4, 8, 16, 128], P('ens', 'tile')
- marine_latent_adjoint: bfloat16 [4, 32, 64, 256], P('ens', None, 'tile')
- grad_force: bfloat16 [128, 256], replicated
- grad_conv: bfloat16 [9, 256], replicated
- grad_gain: bfloat16 [256], replicated
- grad_up: bfloat16 [256, 1024], replicated
- grad_down: bfloat16 [1024, 256], replicated
The draws below stay inside these ranges and needn't reach their ends.
Inputs may be any that keep to these rules, and one draw needn't show every extreme that they name: `intersecting_air_sites`: the index of an atmosphere cell that lies over the ocean cell's own tile: row * 2 + column, with the row among all 8 rows and the column among the 2 atmosphere columns over that tile. `terrain_water_indicator`: 1 marks a sea cell, 0 a land cell.
All inputs are finite; a program needn't handle non-finite values.
Results may differ from the reference program's by a relative error of at most 0.0082.
Values may be sent and summed in bfloat16 or wider, within the bound.
A program may use at most 64 MiB of HBM per device.

```python
import math
import jax
import jax.numpy as jnp
from jax import lax

ACOLS = 2
SUBDIVISION = 4
K = 4
KS = 3
MARINE_DIMENSION = 256
HID = 1024
AW = 384
LINKED_QUANTITY = 128
MEMBERS = 4
ALAT = 8
ALON = 16
OLAT = 32
OCOLS = 8
OLON = 64


def draw_intersecting_air_sites(key, part):
    first_key, second_key = jax.random.split(key)
    base_rows = (jnp.arange(OLAT) // SUBDIVISION).astype(jnp.int32)[None, :, None]
    base_cols = (jnp.arange(OLON) % OCOLS // SUBDIVISION).astype(jnp.int32)[None, None, :]
    row_shift = jax.random.randint(first_key, (K, OLAT, OLON), -1, 2)
    col_shift = jax.random.randint(second_key, (K, OLAT, OLON), -1, 2)
    leading = (jnp.arange(K) == 0)[:, None, None]
    row_shift = jnp.where(leading, 0, row_shift)
    col_shift = jnp.where(leading, 0, col_shift)
    rows = jnp.clip(base_rows + row_shift, 0, ALAT - 1)
    cols = jnp.clip(base_cols + col_shift, 0, ACOLS - 1)
    return (rows * ACOLS + cols).astype(jnp.int32)


def draw_terrain_water_indicator(key, part):
    level_key, coarse_key, fine_key = jax.random.split(key, 3)
    strips = OLON // OCOLS
    level = jax.random.randint(level_key, (strips,), 1, 5)
    column_level = level[jnp.arange(ALON) // ACOLS]
    coarse = jax.random.randint(coarse_key, (ALAT, ALON), 0, 4) < column_level[None, :]
    coarse_fine = jnp.repeat(jnp.repeat(coarse, SUBDIVISION, axis=0), SUBDIVISION, axis=1)
    fine = jax.random.randint(fine_key, (OLAT, OLON), 0, 8) < 7
    return (coarse_fine & fine).astype(jnp.int32)


def plant(drawn, rng, smallest, top_value):
    dims = drawn.shape
    place = [jax.random.randint(jax.random.fold_in(rng, axis), (), 0, dims[axis]) for axis in range(len(dims))]
    drawn = drawn.at[tuple(place)].set(smallest)
    longest = dims.index(max(dims))
    place[longest] = (place[longest] + 1) % dims[longest]
    return drawn.at[tuple(place)].set(top_value)


def levels(rng, shape, shards, low, top_value):
    level, own = 1.0, jax.random.fold_in(rng, 6)
    for dim, shards_of in shards:
        heights = jnp.exp(jax.random.uniform(jax.random.fold_in(own, dim), (shards_of,), jnp.float32, low / len(shards), top_value / len(shards)))
        level = level * jnp.repeat(heights, shape[dim] // shards_of).reshape([-1 if axis == dim else 1 for axis in range(len(shape))])
    return level


def gaussian(rng, extent, width, most, shards=(), dtype=jnp.bfloat16):
    entries = jax.random.normal(rng, extent, jnp.float32) * width
    if len(shards) > 0:
        entries = levels(rng, extent, shards, -0.22, 0.18) * entries
    return jnp.clip(entries, min=-most, max=most).astype(dtype)


def setup_inputs(seed: int = 0) -> dict:
    seeds = jax.random.split(jax.random.key(seed), 14)
    air_latent_array = gaussian(seeds[0], (MEMBERS, ALAT, ALON, AW), 1.0, 6.0, ((0, 4), (1, 8)))
    air_exchange_projection = gaussian(seeds[1], (AW, LINKED_QUANTITY), AW ** -0.5, 0.3125)
    marine_latent_array = gaussian(seeds[2], (MEMBERS, OLAT, OLON, MARINE_DIMENSION), 1.0, 6.0, ((0, 4), (2, 8)))
    driver_projection_matrix = gaussian(seeds[3], (LINKED_QUANTITY, MARINE_DIMENSION), LINKED_QUANTITY ** -0.5, 0.5)
    spatial_kernel_taps = gaussian(seeds[4], (KS * KS, MARINE_DIMENSION), 0.33, 1.5, (), jnp.float32)
    layernorm_multiplier = jnp.clip(1.0 + 0.15 * jax.random.normal(seeds[5], (MARINE_DIMENSION,), jnp.float32), 0.25, 1.75)
    pointwise_widen_matrix = gaussian(seeds[6], (MARINE_DIMENSION, HID), MARINE_DIMENSION ** -0.5, 0.375)
    pointwise_shrink_matrix = gaussian(seeds[7], (HID, MARINE_DIMENSION), HID ** -0.5, 0.1875)
    thermal_projection_matrix = gaussian(seeds[8], (MARINE_DIMENSION, LINKED_QUANTITY), MARINE_DIMENSION ** -0.5, 0.375)
    intersecting_air_sites = draw_intersecting_air_sites(jax.random.fold_in(seeds[13], 71), 0)
    margin_multiplier = plant(jax.random.randint(seeds[10], (K, OLAT, OLON), 1, 9), jax.random.fold_in(seeds[10], 1), 1, 8).astype(jnp.int32)
    terrain_water_indicator = draw_terrain_water_indicator(jax.random.fold_in(seeds[13], 71), 0)
    marine_successor_adjoint = gaussian(seeds[12], (MEMBERS, OLAT, OLON, MARINE_DIMENSION), 1.0, 6.0, ((0, 4), (2, 8)))
    return {"air_latent_array": air_latent_array, "air_exchange_projection": air_exchange_projection, "marine_latent_array": marine_latent_array, "driver_projection_matrix": driver_projection_matrix, "spatial_kernel_taps": spatial_kernel_taps, "layernorm_multiplier": layernorm_multiplier, "pointwise_widen_matrix": pointwise_widen_matrix, "pointwise_shrink_matrix": pointwise_shrink_matrix, "thermal_projection_matrix": thermal_projection_matrix, "intersecting_air_sites": intersecting_air_sites, "margin_multiplier": margin_multiplier, "terrain_water_indicator": terrain_water_indicator, "marine_successor_adjoint": marine_successor_adjoint}


def layer_norm(values, gain):
    centred = values - lax.optimization_barrier(jnp.mean(values, axis=-1, keepdims=True))
    spread = lax.optimization_barrier(jnp.mean(centred * centred, axis=-1, keepdims=True))
    return centred * lax.rsqrt(spread + 1e-06) * gain

def regrid(flat_fluxes, cell_ids, margin):
    picked = jnp.take(flat_fluxes, cell_ids, axis=0).astype(jnp.float32)
    factor = margin.astype(jnp.float32)
    weighted = lax.optimization_barrier(jnp.sum(factor[..., None] * picked, axis=0))
    return (weighted / lax.optimization_barrier(jnp.sum(factor, axis=0))[..., None]).astype(jnp.bfloat16)

def marine_update_kernel(marine_present_latent, marine_driver_input, latent_adjoint, water_indicator_real, driver_projection_matrix, spatial_kernel_taps, layernorm_multiplier, pointwise_widen_matrix, pointwise_shrink_matrix, thermal_projection_matrix, haloed_latent, haloed_derivative):
    horizontal_sum_result, vertical_sum_result, feature_dimension = marine_present_latent.shape
    reach = KS // 2
    forcing_flat = marine_driver_input.reshape(-1, marine_driver_input.shape[-1])
    pushed = jnp.dot(forcing_flat, driver_projection_matrix, preferred_element_type=jnp.float32).reshape(horizontal_sum_result, vertical_sum_result, feature_dimension)
    mixed = (marine_present_latent.astype(jnp.float32) + pushed).astype(jnp.bfloat16)
    padded = jnp.pad(haloed_latent(mixed), ((reach, reach), (0, 0), (0, 0))).astype(jnp.float32)
    conv_out = jnp.zeros((horizontal_sum_result, vertical_sum_result, feature_dimension), jnp.float32)
    for row_off in range(KS):
        for col_off in range(KS):
            conv_out = conv_out + spatial_kernel_taps[row_off * KS + col_off] * padded[row_off:row_off + horizontal_sum_result, col_off:col_off + vertical_sum_result]
    normed_f, pull_norm = jax.vjp(layer_norm, conv_out.reshape(-1, feature_dimension), layernorm_multiplier)
    normed = normed_f.astype(jnp.bfloat16)
    hidden_pre = jnp.dot(normed, pointwise_widen_matrix, preferred_element_type=jnp.float32)
    hidden_f, pull_gelu = jax.vjp(jax.nn.gelu, hidden_pre)
    hidden = hidden_f.astype(jnp.bfloat16)
    mlp_out = jnp.dot(hidden, pointwise_shrink_matrix, preferred_element_type=jnp.float32)
    sea_column = water_indicator_real.reshape(-1, 1)
    marine_successor_latent = (sea_column * (mixed.reshape(-1, feature_dimension).astype(jnp.float32) + mlp_out)).astype(jnp.bfloat16)
    thermal_highres_field = jnp.dot(marine_successor_latent, thermal_projection_matrix, preferred_element_type=jnp.float32)
    thermal_highres_field = thermal_highres_field.reshape(horizontal_sum_result // SUBDIVISION, SUBDIVISION, vertical_sum_result // SUBDIVISION, SUBDIVISION, thermal_highres_field.shape[-1])
    marine_site_number = lax.optimization_barrier(jnp.sum(water_indicator_real.reshape(horizontal_sum_result // SUBDIVISION, SUBDIVISION, vertical_sum_result // SUBDIVISION, SUBDIVISION), axis=(1, 3)))
    thermal_lowres_field = (lax.optimization_barrier(jnp.sum(thermal_highres_field, axis=(1, 3))) / jnp.maximum(marine_site_number, 1.0)[..., None]).astype(jnp.bfloat16)
    masked_cot = (sea_column * latent_adjoint.reshape(-1, feature_dimension).astype(jnp.float32)).astype(jnp.bfloat16)
    grad_down = jnp.dot(hidden.T, masked_cot, preferred_element_type=jnp.float32)
    hidden_cot = jnp.dot(masked_cot, pointwise_shrink_matrix.T, preferred_element_type=jnp.float32)
    pre_cot = pull_gelu(hidden_cot)[0].astype(jnp.bfloat16)
    grad_up = jnp.dot(normed.T, pre_cot, preferred_element_type=jnp.float32)
    normed_cot = jnp.dot(pre_cot, pointwise_widen_matrix.T, preferred_element_type=jnp.float32)
    conv_cot, grad_gain = pull_norm(normed_cot)
    conv_cot = conv_cot.reshape(horizontal_sum_result, vertical_sum_result, feature_dimension)
    tap_grads = []
    for row_off in range(KS):
        for col_off in range(KS):
            tap_grads.append(lax.optimization_barrier(jnp.sum(conv_cot * padded[row_off:row_off + horizontal_sum_result, col_off:col_off + vertical_sum_result], axis=(0, 1))))
    grad_padded = jnp.pad(haloed_derivative(conv_cot), ((reach, reach), (0, 0), (0, 0)))
    back = masked_cot.astype(jnp.float32).reshape(horizontal_sum_result, vertical_sum_result, feature_dimension)
    for row_off in range(KS):
        for col_off in range(KS):
            row_from = KS - 1 - row_off
            col_from = KS - 1 - col_off
            back = back + spatial_kernel_taps[row_off * KS + col_off] * grad_padded[row_from:row_from + horizontal_sum_result, col_from:col_from + vertical_sum_result]
    marine_latent_adjoint = back.astype(jnp.bfloat16)
    grad_force = jnp.dot(forcing_flat.T, marine_latent_adjoint.reshape(-1, feature_dimension), preferred_element_type=jnp.float32)
    derivative_sequence = (grad_force, jnp.stack(tap_grads), grad_gain, grad_up, grad_down)
    return (marine_successor_latent.reshape(horizontal_sum_result, vertical_sum_result, feature_dimension), thermal_lowres_field, marine_latent_adjoint, derivative_sequence)

def periodic_extended_lanes(values):
    reach = KS // 2
    return jnp.concatenate([values[:, -reach:], values, values[:, :reach]], axis=1)

def reference(air_latent_array, air_exchange_projection, marine_latent_array, driver_projection_matrix, spatial_kernel_taps, layernorm_multiplier, pointwise_widen_matrix, pointwise_shrink_matrix, thermal_projection_matrix, intersecting_air_sites, margin_multiplier, terrain_water_indicator, marine_successor_adjoint):
    strip_of = (jnp.arange(OLON) // OCOLS).astype(jnp.int32)
    global_ids = (intersecting_air_sites // ACOLS * ALON + strip_of[None, None, :] * ACOLS + intersecting_air_sites % ACOLS).astype(jnp.int32)
    water_indicator_real = terrain_water_indicator.astype(jnp.float32)

    def sample_replica(member_args):
        atmos, marine_present_latent, latent_adjoint = member_args
        fluxes = jnp.dot(atmos.reshape(-1, AW), air_exchange_projection, preferred_element_type=jnp.float32).astype(jnp.bfloat16)
        marine_driver_input = regrid(fluxes, global_ids, margin_multiplier)
        return marine_update_kernel(marine_present_latent, marine_driver_input, latent_adjoint, water_indicator_real, driver_projection_matrix, spatial_kernel_taps, layernorm_multiplier, pointwise_widen_matrix, pointwise_shrink_matrix, thermal_projection_matrix, periodic_extended_lanes, periodic_extended_lanes)
    successor_latent_tensor, thermal_tensor, derivative_tensor, derivative_sequence = lax.map(sample_replica, (air_latent_array, marine_latent_array, marine_successor_adjoint))
    grad_scale = 1.0 / math.sqrt(MEMBERS * OLAT * OLON)
    accumulated_result = [(lax.optimization_barrier(jnp.sum(values, axis=0)) * grad_scale).astype(jnp.bfloat16) for values in derivative_sequence]
    return (successor_latent_tensor, thermal_tensor, derivative_tensor, accumulated_result[0], accumulated_result[1], accumulated_result[2], accumulated_result[3], accumulated_result[4])
```

```python
import functools
import math

import jax
import jax.numpy as jnp
from jax import lax
from jax.experimental import pallas as pl
from jax.experimental.pallas import tpu as pltpu
from jax.sharding import PartitionSpec as P

SUBDIVISION = 4
KS = 3
LANES = 128
SLAB = 8
MESH = pl.DeviceIdType.MESH


def pack_plan(shapes):
    plan, at = [], 0
    for which, (rows, cols) in enumerate(shapes):
        for col in range(0, cols, LANES):
            plan.append((which, col, at, rows))
            at += rows
    return plan, at


def reduce_kernel(
    scale,
    ne,
    nt,
    rows,
    plan,
    used,
    up_ref,
    down_ref,
    force_ref,
    small_ref,
    therm_ref,
    up_out,
    down_out,
    force_out,
    small_out,
    therm_out,
    packed,
    from_core,
    halves,
    from_ens,
    part,
    from_z,
    whole,
    therm_in,
    t_send,
    t_recv,
    a_send,
    a_recv,
    b_send,
    b_recv,
    c_send,
    c_recv,
    d_send,
    d_recv,
    e_send,
    e_recv,
    f_send,
    f_recv,
):
    nz = nt // 2
    block = nz * rows
    half = ne * block
    ens = lax.axis_index("ens")
    tile = lax.axis_index("tile")
    z = tile // 2
    core = tile % 2
    other = 1 - core
    mate = {"tile": z * 2 + other}

    def send(src, dst, s_sem, r_sem, device):
        copy = pltpu.make_async_remote_copy(
            src_ref=src,
            dst_ref=dst,
            send_sem=s_sem,
            recv_sem=r_sem,
            device_id=device,
            device_id_type=MESH,
        )
        copy.start()
        return copy

    barrier = pltpu.get_barrier_semaphore()
    for o in range(1, nt):
        pl.semaphore_signal(
            barrier, inc=1, device_id={"tile": (tile + o) % nt}, device_id_type=MESH
        )
    for o in range(1, ne):
        pl.semaphore_signal(
            barrier, inc=1, device_id={"ens": (ens + o) % ne}, device_id_type=MESH
        )

    ins = (up_ref, down_ref, force_ref, small_ref)
    for which, col, at, count in plan:
        packed[at : at + count, :] = ins[which][:, col : col + LANES].astype(jnp.bfloat16)
    if used < 2 * half:
        packed[used : 2 * half, :] = jnp.zeros((2 * half - used, LANES), jnp.bfloat16)
    pl.semaphore_wait(barrier, nt - 1 + ne - 1)

    def at_block(h, e):
        return pl.ds(pl.multiple_of((h * ne + e) * block, 16), block)

    order = list(range(1, ne)) + [0]
    a_copies = []
    for o in order:
        e = (ens + o) % ne
        a_copies.append(
            send(
                packed.at[at_block(other, e)],
                from_core.at[o],
                a_send.at[o],
                a_recv.at[o],
                mate,
            )
        )
    t_copies = []
    for o in range(1, nt):
        to = (tile + o) % nt
        t_copies.append(
            send(
                therm_ref.at[to],
                therm_in.at[o],
                t_send.at[o],
                t_recv.at[o],
                {"tile": to},
            )
        )
    b_copies = []
    for o, copy in zip(order, a_copies):
        e = (ens + o) % ne
        copy.wait_recv()
        halves[o] = (
            packed[at_block(core, e), :].astype(jnp.float32) + from_core[o].astype(jnp.float32)
        ).astype(jnp.bfloat16)
        if o:
            b_copies.append(
                send(halves.at[o], from_ens.at[o], b_send.at[o], b_recv.at[o], {"ens": e})
            )
    total = halves[0].astype(jnp.float32)
    for o, copy in zip(range(1, ne), b_copies):
        copy.wait_recv()
        total = total + from_ens[o].astype(jnp.float32)
    part[...] = total.astype(jnp.bfloat16)

    def at_chunk(where):
        return pl.ds(pl.multiple_of(where * rows, 16), rows)

    c_copies = []
    for o in range(1, nz):
        to = (z + o) % nz
        c_copies.append(
            send(
                part.at[at_chunk(to)],
                from_z.at[o],
                c_send.at[o],
                c_recv.at[o],
                {"tile": to * 2 + core},
            )
        )
    mine = part[at_chunk(z), :].astype(jnp.float32)
    for o, copy in zip(range(1, nz), c_copies):
        copy.wait_recv()
        mine = mine + from_z[o].astype(jnp.float32)
    spot = (core * ne + ens) * nz + z
    whole[at_chunk(spot), :] = (mine * scale).astype(jnp.bfloat16)
    d_copies = []
    for o in range(1, nz):
        to = (z + o) % nz
        d_copies.append(
            send(
                whole.at[at_chunk(spot)],
                whole.at[at_chunk(spot)],
                d_send.at[o],
                d_recv.at[o],
                {"tile": to * 2 + core},
            )
        )
    for copy in d_copies:
        copy.wait_recv()
    e_copies = []
    for o in range(1, ne):
        e_copies.append(
            send(
                whole.at[at_block(core, ens)],
                whole.at[at_block(core, ens)],
                e_send.at[o],
                e_recv.at[o],
                {"ens": (ens + o) % ne},
            )
        )
    f_copies = [
        send(
            whole.at[at_block(core, ens)],
            whole.at[at_block(core, ens)],
            f_send.at[0],
            f_recv.at[0],
            mate,
        )
    ]
    for o, copy in zip(range(1, ne), e_copies):
        copy.wait_recv()
        e = (ens + ne - o) % ne
        f_copies.append(
            send(
                whole.at[at_block(core, e)],
                whole.at[at_block(core, e)],
                f_send.at[o],
                f_recv.at[o],
                mate,
            )
        )
    therm_out[tile] = therm_ref[tile]
    for o, copy in zip(range(1, nt), t_copies):
        copy.wait_recv()
        therm_out[(tile + nt - o) % nt] = therm_in[o]
    for copy in f_copies:
        copy.wait_recv()
    for copy in a_copies + t_copies + b_copies + c_copies + d_copies + e_copies + f_copies:
        copy.wait_send()
    outs = (up_out, down_out, force_out, small_out)
    for which, col, at, count in plan:
        outs[which][:, col : col + LANES] = whole[at : at + count, :]


def reduce_gradients(up, down, force, small, therm, scale):
    ne, nt = lax.axis_size("ens"), lax.axis_size("tile")
    nz = nt // 2
    plan, used = pack_plan([up.shape, down.shape, force.shape, small.shape])
    rows = -(-used // (2 * ne * nz * 16)) * 16
    block = nz * rows
    bf16 = jnp.bfloat16
    dma = pltpu.SemaphoreType.DMA
    vmem = pl.BlockSpec(memory_space=pltpu.VMEM)
    return pl.pallas_call(
        functools.partial(reduce_kernel, scale, ne, nt, rows, plan, used),
        out_shape=[
            jax.ShapeDtypeStruct(up.shape, bf16),
            jax.ShapeDtypeStruct(down.shape, bf16),
            jax.ShapeDtypeStruct(force.shape, bf16),
            jax.ShapeDtypeStruct(small.shape, bf16),
            jax.ShapeDtypeStruct(therm.shape, therm.dtype),
        ],
        in_specs=[vmem] * 5,
        out_specs=[vmem] * 5,
        scratch_shapes=[
            pltpu.VMEM((2 * ne * block, LANES), bf16),
            pltpu.VMEM((ne, block, LANES), bf16),
            pltpu.VMEM((ne, block, LANES), bf16),
            pltpu.VMEM((ne, block, LANES), bf16),
            pltpu.VMEM((block, LANES), bf16),
            pltpu.VMEM((nz, rows, LANES), bf16),
            pltpu.VMEM((2 * ne * block, LANES), bf16),
            pltpu.VMEM(therm.shape, therm.dtype),
        ]
        + [dma((nt,)), dma((nt,))]
        + [dma((ne,)), dma((ne,))] * 2
        + [dma((nz,)), dma((nz,))] * 2
        + [dma((ne,)), dma((ne,))] * 2,
        compiler_params=pltpu.CompilerParams(collective_id=1, has_side_effects=True),
        name="reduce_gradients",
    )(up, down, force, small, therm)


def extended(cells, sides, width):
    for axis, dim in sides:
        count = lax.axis_size(axis)
        head = lax.slice_in_dim(cells, 0, width, axis=dim)
        tail = lax.slice_in_dim(cells, cells.shape[dim] - width, cells.shape[dim], axis=dim)
        cells = jnp.concatenate(
            [
                lax.ppermute(tail, axis, [(i, (i + 1) % count) for i in range(count)]),
                cells,
                lax.ppermute(head, axis, [((i + 1) % count, i) for i in range(count)]),
            ],
            axis=dim,
        )
    return cells


def layer_norm(values, gain):
    centred = values - jnp.mean(values, axis=-1, keepdims=True)
    spread = jnp.mean(centred * centred, axis=-1, keepdims=True)
    return centred * lax.rsqrt(spread + 1e-06) * gain


def regrid(flat_fluxes, cell_ids, margin):
    picked = jnp.take(flat_fluxes, cell_ids, axis=0).astype(jnp.float32)
    factor = margin.astype(jnp.float32)
    weighted = jnp.sum(factor[..., None] * picked, axis=0)
    return (weighted / jnp.sum(factor, axis=0)[..., None]).astype(jnp.bfloat16)


def marine_update_kernel(
    marine_present_latent,
    marine_driver_input,
    latent_adjoint,
    water_indicator_real,
    driver_projection_matrix,
    spatial_kernel_taps,
    layernorm_multiplier,
    pointwise_widen_matrix,
    pointwise_shrink_matrix,
    thermal_projection_matrix,
    haloed_latent,
    haloed_derivative,
):
    horizontal_sum_result, vertical_sum_result, feature_dimension = marine_present_latent.shape
    reach = KS // 2
    forcing_flat = marine_driver_input.reshape(-1, marine_driver_input.shape[-1])
    pushed = jnp.dot(
        forcing_flat, driver_projection_matrix, preferred_element_type=jnp.float32
    ).reshape(horizontal_sum_result, vertical_sum_result, feature_dimension)
    mixed = (marine_present_latent.astype(jnp.float32) + pushed).astype(jnp.bfloat16)
    padded = jnp.pad(haloed_latent(mixed), ((reach, reach), (0, 0), (0, 0))).astype(jnp.float32)
    conv_out = jnp.zeros(
        (horizontal_sum_result, vertical_sum_result, feature_dimension), jnp.float32
    )
    for row_off in range(KS):
        for col_off in range(KS):
            conv_out = (
                conv_out
                + spatial_kernel_taps[row_off * KS + col_off]
                * padded[
                    row_off : row_off + horizontal_sum_result,
                    col_off : col_off + vertical_sum_result,
                ]
            )
    normed_f, pull_norm = jax.vjp(
        layer_norm, conv_out.reshape(-1, feature_dimension), layernorm_multiplier
    )
    normed = normed_f.astype(jnp.bfloat16)
    hidden_pre = jnp.dot(normed, pointwise_widen_matrix, preferred_element_type=jnp.float32)
    hidden_f, pull_gelu = jax.vjp(jax.nn.gelu, hidden_pre)
    hidden = hidden_f.astype(jnp.bfloat16)
    mlp_out = jnp.dot(hidden, pointwise_shrink_matrix, preferred_element_type=jnp.float32)
    sea_column = water_indicator_real.reshape(-1, 1)
    marine_successor_latent = (
        sea_column * (mixed.reshape(-1, feature_dimension).astype(jnp.float32) + mlp_out)
    ).astype(jnp.bfloat16)
    thermal_highres_field = jnp.dot(
        marine_successor_latent, thermal_projection_matrix, preferred_element_type=jnp.float32
    )
    thermal_highres_field = thermal_highres_field.reshape(
        horizontal_sum_result // SUBDIVISION,
        SUBDIVISION,
        vertical_sum_result // SUBDIVISION,
        SUBDIVISION,
        thermal_highres_field.shape[-1],
    )
    marine_site_number = jnp.sum(
        water_indicator_real.reshape(
            horizontal_sum_result // SUBDIVISION,
            SUBDIVISION,
            vertical_sum_result // SUBDIVISION,
            SUBDIVISION,
        ),
        axis=(1, 3),
    )
    thermal_lowres_field = (
        jnp.sum(thermal_highres_field, axis=(1, 3))
        / jnp.maximum(marine_site_number, 1.0)[..., None]
    ).astype(jnp.bfloat16)
    masked_cot = (
        sea_column * latent_adjoint.reshape(-1, feature_dimension).astype(jnp.float32)
    ).astype(jnp.bfloat16)
    grad_down = jnp.dot(hidden.T, masked_cot, preferred_element_type=jnp.float32)
    hidden_cot = jnp.dot(masked_cot, pointwise_shrink_matrix.T, preferred_element_type=jnp.float32)
    pre_cot = pull_gelu(hidden_cot)[0].astype(jnp.bfloat16)
    grad_up = jnp.dot(normed.T, pre_cot, preferred_element_type=jnp.float32)
    normed_cot = jnp.dot(pre_cot, pointwise_widen_matrix.T, preferred_element_type=jnp.float32)
    conv_cot, grad_gain = pull_norm(normed_cot)
    conv_cot = conv_cot.reshape(horizontal_sum_result, vertical_sum_result, feature_dimension)
    tap_grads = []
    for row_off in range(KS):
        for col_off in range(KS):
            tap_grads.append(
                jnp.sum(
                    conv_cot
                    * padded[
                        row_off : row_off + horizontal_sum_result,
                        col_off : col_off + vertical_sum_result,
                    ],
                    axis=(0, 1),
                )
            )
    grad_padded = jnp.pad(haloed_derivative(conv_cot), ((reach, reach), (0, 0), (0, 0)))
    back = masked_cot.astype(jnp.float32).reshape(
        horizontal_sum_result, vertical_sum_result, feature_dimension
    )
    for row_off in range(KS):
        for col_off in range(KS):
            row_from = KS - 1 - row_off
            col_from = KS - 1 - col_off
            back = (
                back
                + spatial_kernel_taps[row_off * KS + col_off]
                * grad_padded[
                    row_from : row_from + horizontal_sum_result,
                    col_from : col_from + vertical_sum_result,
                ]
            )
    marine_latent_adjoint = back.astype(jnp.bfloat16)
    grad_force = jnp.dot(
        forcing_flat.T,
        marine_latent_adjoint.reshape(-1, feature_dimension),
        preferred_element_type=jnp.float32,
    )
    derivative_sequence = (grad_force, jnp.stack(tap_grads), grad_gain, grad_up, grad_down)
    return (
        marine_successor_latent.reshape(
            horizontal_sum_result, vertical_sum_result, feature_dimension
        ),
        thermal_lowres_field,
        marine_latent_adjoint,
        derivative_sequence,
    )


def pad_state_cols(values):
    return extended(values, (("tile", 1),), KS // 2)


def pad_grad_cols(values):
    return extended(values, (("tile", 1),), KS // 2)


def body(
    air_latent_array,
    air_exchange_projection,
    marine_latent_array,
    driver_projection_matrix,
    spatial_kernel_taps,
    layernorm_multiplier,
    pointwise_widen_matrix,
    pointwise_shrink_matrix,
    thermal_projection_matrix,
    intersecting_air_sites,
    margin_multiplier,
    terrain_water_indicator,
    marine_successor_adjoint,
):
    band = air_latent_array[0]
    band_rows, band_cols, atmos_width = band.shape
    fluxes = jnp.dot(
        band.reshape(-1, atmos_width), air_exchange_projection, preferred_element_type=jnp.float32
    ).astype(jnp.bfloat16)
    fluxes = fluxes.reshape(band_rows, band_cols, fluxes.shape[-1])
    strip = lax.all_to_all(fluxes, "tile", split_axis=1, concat_axis=0, tiled=True)
    marine_driver_input = regrid(
        strip.reshape(-1, strip.shape[-1]), intersecting_air_sites, margin_multiplier
    )
    water_indicator_real = terrain_water_indicator.astype(jnp.float32)
    marine_successor_latent, thermal_lowres_field, marine_latent_adjoint, derivative_sequence = (
        marine_update_kernel(
            marine_latent_array[0],
            marine_driver_input,
            marine_successor_adjoint[0],
            water_indicator_real,
            driver_projection_matrix,
            spatial_kernel_taps,
            layernorm_multiplier,
            pointwise_widen_matrix,
            pointwise_shrink_matrix,
            thermal_projection_matrix,
            pad_state_cols,
            pad_grad_cols,
        )
    )
    cell_total = (
        lax.axis_size("ens")
        * lax.axis_size("tile")
        * marine_successor_latent.shape[0]
        * marine_successor_latent.shape[1]
    )
    grad_scale = 1.0 / math.sqrt(cell_total)
    grad_force, grad_conv, grad_gain, grad_up, grad_down = derivative_sequence
    taps, features = grad_conv.shape
    small = jnp.pad(
        jnp.concatenate([grad_conv, grad_gain.reshape(1, features)]),
        ((0, -(taps + 1) % 16), (0, 0)),
    )
    tiles, columns, quantity = thermal_lowres_field.shape
    therm = jnp.pad(
        thermal_lowres_field.astype(jnp.float32), ((0, 0), (0, SLAB - columns), (0, 0))
    )
    up, down, force, small, therm = reduce_gradients(
        grad_up, grad_down, grad_force, small, therm, grad_scale
    )
    thermal_strip_slice = (
        therm[:, :columns].reshape(1, tiles * columns, quantity).astype(jnp.bfloat16)
    )
    return (
        marine_successor_latent[None],
        thermal_strip_slice[None],
        marine_latent_adjoint[None],
        force,
        small[:taps],
        small[taps],
        up,
        down,
    )


def solution(mesh):
    return jax.shard_map(
        body,
        mesh=mesh,
        in_specs=(
            P("ens", "tile", None, None),
            P(),
            P("ens", None, "tile", None),
            P(),
            P(),
            P(),
            P(),
            P(),
            P(),
            P(None, None, "tile"),
            P(None, None, "tile"),
            P(None, "tile"),
            P("ens", None, "tile", None),
        ),
        out_specs=(
            P("ens", None, "tile", None),
            P("ens", "tile", None, None),
            P("ens", None, "tile", None),
            P(),
            P(),
            P(),
            P(),
            P(),
        ),
        check_vma=False,
    )
```

```python
import functools
import math

import jax
import jax.numpy as jnp
from jax import lax
from jax.experimental import pallas as pl
from jax.experimental.pallas import tpu as pltpu
from jax.sharding import PartitionSpec as P

SUBDIVISION = 4
KS = 3
LANES = 128
SLABS = 3
MESH = pl.DeviceIdType.MESH


def pack_plan(shapes):
    plan, at = [], 0
    for which, (rows, cols) in enumerate(shapes):
        for col in range(0, cols, LANES):
            plan.append((which, col, at, rows))
            at += rows
    return plan, at


def reduce_kernel(
    scale,
    ne,
    nt,
    rows,
    plan,
    used,
    up_ref,
    down_ref,
    force_ref,
    conv_ref,
    gain_ref,
    therm_ref,
    whole,
    therm_out,
    small,
    packed,
    from_core,
    halves,
    from_ens,
    part,
    from_z,
    therm_in,
    t_send,
    t_recv,
    a_send,
    a_recv,
    b_send,
    b_recv,
    c_send,
    c_recv,
    d_send,
    d_recv,
    e_send,
    e_recv,
    f_send,
    f_recv,
):
    nz = nt // 2
    block = nz * rows
    slab = 2 * ne * block
    ens = lax.axis_index("ens")
    tile = lax.axis_index("tile")
    z = tile // 2
    core = tile % 2
    other = 1 - core
    mate = {"tile": z * 2 + other}

    def send(src, dst, s_sem, r_sem, device):
        copy = pltpu.make_async_remote_copy(
            src_ref=src,
            dst_ref=dst,
            send_sem=s_sem,
            recv_sem=r_sem,
            device_id=device,
            device_id_type=MESH,
        )
        copy.start()
        return copy

    def at_block(s, h, e):
        return pl.ds(pl.multiple_of(s * slab + (h * ne + e) * block, 16), block)

    def at_chunk(where):
        return pl.ds(pl.multiple_of(where * rows, 16), rows)

    barrier = pltpu.get_barrier_semaphore()
    for o in range(1, nt):
        pl.semaphore_signal(
            barrier, inc=1, device_id={"tile": (tile + o) % nt}, device_id_type=MESH
        )
    for o in range(1, ne):
        pl.semaphore_signal(
            barrier, inc=1, device_id={"ens": (ens + o) % ne}, device_id_type=MESH
        )

    taps = conv_ref.shape[0]
    small[...] = jnp.zeros_like(small)
    small[0:taps, :] = conv_ref[...]
    small[taps : taps + 1, :] = gain_ref[...]
    ins = (up_ref, down_ref, force_ref, small)
    if used < SLABS * slab:
        packed[used : SLABS * slab, :] = jnp.zeros((SLABS * slab - used, LANES), jnp.bfloat16)

    order = list(range(1, ne)) + [0]
    a_copies = [[] for _ in range(SLABS)]

    def send_slab(s):
        for o in order:
            e = (ens + o) % ne
            a_copies[s].append(
                send(
                    packed.at[at_block(s, other, e)],
                    from_core.at[s, o],
                    a_send.at[s, o],
                    a_recv.at[s, o],
                    mate,
                )
            )

    ready = 0
    for which, col, at, count in plan:
        packed[at : at + count, :] = ins[which][:, col : col + LANES].astype(jnp.bfloat16)
        while ready < SLABS and at + count >= min((ready + 1) * slab, used):
            if ready == 0:
                pl.semaphore_wait(barrier, nt - 1 + ne - 1)
            send_slab(ready)
            ready += 1

    t_copies = []
    for o in range(1, nt):
        to = (tile + o) % nt
        t_copies.append(
            send(
                therm_ref.at[to],
                therm_in.at[o],
                t_send.at[o],
                t_recv.at[o],
                {"tile": to},
            )
        )
    b_copies = [[] for _ in range(SLABS)]
    for s in range(SLABS):
        for o, copy in zip(order, a_copies[s]):
            e = (ens + o) % ne
            copy.wait_recv()
            halves[s, o] = (
                packed[at_block(s, core, e), :].astype(jnp.float32)
                + from_core[s, o].astype(jnp.float32)
            ).astype(jnp.bfloat16)
            if o:
                b_copies[s].append(
                    send(
                        halves.at[s, o],
                        from_ens.at[s, o],
                        b_send.at[s, o],
                        b_recv.at[s, o],
                        {"ens": e},
                    )
                )
    c_copies = [[] for _ in range(SLABS)]
    for s in range(SLABS):
        total = halves[s, 0].astype(jnp.float32)
        for o, copy in zip(range(1, ne), b_copies[s]):
            copy.wait_recv()
            total = total + from_ens[s, o].astype(jnp.float32)
        part[s] = total.astype(jnp.bfloat16)
        for o in range(1, nz):
            to = (z + o) % nz
            c_copies[s].append(
                send(
                    part.at[s, at_chunk(to)],
                    from_z.at[s, o],
                    c_send.at[s, o],
                    c_recv.at[s, o],
                    {"tile": to * 2 + core},
                )
            )
    d_copies = [[] for _ in range(SLABS)]
    for s in range(SLABS):
        mine = part[s, at_chunk(z), :].astype(jnp.float32)
        for o, copy in zip(range(1, nz), c_copies[s]):
            copy.wait_recv()
            mine = mine + from_z[s, o].astype(jnp.float32)
        spot = at_chunk(((s * 2 + core) * ne + ens) * nz + z)
        whole[spot, :] = (mine * scale).astype(jnp.bfloat16)
        for o in range(1, nz):
            to = (z + o) % nz
            d_copies[s].append(
                send(
                    whole.at[spot],
                    whole.at[spot],
                    d_send.at[s, o],
                    d_recv.at[s, o],
                    {"tile": to * 2 + core},
                )
            )
    e_copies = [[] for _ in range(SLABS)]
    f_copies = []
    for s in range(SLABS):
        for copy in d_copies[s]:
            copy.wait_recv()
        own = at_block(s, core, ens)
        for o in range(1, ne):
            e_copies[s].append(
                send(
                    whole.at[own],
                    whole.at[own],
                    e_send.at[s, o],
                    e_recv.at[s, o],
                    {"ens": (ens + o) % ne},
                )
            )
        f_copies.append(send(whole.at[own], whole.at[own], f_send.at[s, 0], f_recv.at[s, 0], mate))
    for s in range(SLABS):
        for o, copy in zip(range(1, ne), e_copies[s]):
            copy.wait_recv()
            theirs = at_block(s, core, (ens + ne - o) % ne)
            f_copies.append(
                send(whole.at[theirs], whole.at[theirs], f_send.at[s, o], f_recv.at[s, o], mate)
            )
    therm_out[tile] = therm_ref[tile]
    for o, copy in zip(range(1, nt), t_copies):
        copy.wait_recv()
        therm_out[(tile + nt - o) % nt] = therm_in[o]
    for copy in f_copies:
        copy.wait_recv()
    sent = t_copies + f_copies
    for group in (a_copies, b_copies, c_copies, d_copies, e_copies):
        for copies in group:
            sent = sent + copies
    for copy in sent:
        copy.wait_send()


def unpack_kernel(
    plan, whole, therm, up_out, down_out, force_out, conv_out, gain_out, therm_out, strip, sems
):
    outs = (up_out, down_out, force_out)
    copies = []
    for i, (which, col, at, count) in enumerate(plan):
        if which < len(outs):
            copies.append(
                pltpu.make_async_copy(
                    whole.at[at : at + count, :],
                    outs[which].at[:, col : col + LANES],
                    sems.at[i],
                )
            )
            copies[-1].start()
    taps = conv_out.shape[0]
    for which, col, at, count in plan:
        if which == len(outs):
            rows = whole[at : at + count, :].astype(jnp.float32)
            conv_out[:, col : col + LANES] = rows[:taps].astype(jnp.bfloat16)
            gain_out[:, col : col + LANES] = rows[taps : taps + 1].astype(jnp.bfloat16)
    tiles, columns, _ = therm.shape
    for t in range(tiles):
        strip[t * columns : (t + 1) * columns, :] = therm[t]
    therm_out[0] = strip[...].astype(jnp.bfloat16)
    for copy in copies:
        copy.wait()


def reduce_gradients(up, down, force, conv, gain, therm, scale):
    ne, nt = lax.axis_size("ens"), lax.axis_size("tile")
    nz = nt // 2
    taps, features = conv.shape
    small_rows = -(-(taps + 1) // 16) * 16
    plan, used = pack_plan([up.shape, down.shape, force.shape, (small_rows, features)])
    rows = -(-used // (SLABS * 2 * ne * nz * 16)) * 16
    block = nz * rows
    bf16 = jnp.bfloat16
    dma = pltpu.SemaphoreType.DMA
    vmem = pl.BlockSpec(memory_space=pltpu.VMEM)
    anywhere = pl.BlockSpec(memory_space=pl.ANY)
    tiles, columns, quantity = therm.shape
    whole, therm = pl.pallas_call(
        functools.partial(reduce_kernel, scale, ne, nt, rows, plan, used),
        out_shape=[
            jax.ShapeDtypeStruct((SLABS * 2 * ne * block, LANES), bf16),
            jax.ShapeDtypeStruct(therm.shape, therm.dtype),
        ],
        in_specs=[vmem] * 6,
        out_specs=[vmem] * 2,
        scratch_shapes=[
            pltpu.VMEM((small_rows, features), jnp.float32),
            pltpu.VMEM((SLABS * 2 * ne * block, LANES), bf16),
            pltpu.VMEM((SLABS, ne, block, LANES), bf16),
            pltpu.VMEM((SLABS, ne, block, LANES), bf16),
            pltpu.VMEM((SLABS, ne, block, LANES), bf16),
            pltpu.VMEM((SLABS, block, LANES), bf16),
            pltpu.VMEM((SLABS, nz, rows, LANES), bf16),
            pltpu.VMEM(therm.shape, therm.dtype),
        ]
        + [dma((nt,)), dma((nt,))]
        + [dma((SLABS, ne)), dma((SLABS, ne))] * 2
        + [dma((SLABS, nz)), dma((SLABS, nz))] * 2
        + [dma((SLABS, ne)), dma((SLABS, ne))] * 2,
        compiler_params=pltpu.CompilerParams(collective_id=1, has_side_effects=True),
        name="reduce_gradients",
    )(up, down, force, conv, gain, therm)
    return pl.pallas_call(
        functools.partial(unpack_kernel, plan),
        out_shape=[
            jax.ShapeDtypeStruct(up.shape, bf16),
            jax.ShapeDtypeStruct(down.shape, bf16),
            jax.ShapeDtypeStruct(force.shape, bf16),
            jax.ShapeDtypeStruct(conv.shape, bf16),
            jax.ShapeDtypeStruct(gain.shape, bf16),
            jax.ShapeDtypeStruct((1, tiles * columns, quantity), bf16),
        ],
        in_specs=[vmem] * 2,
        out_specs=[anywhere] * 3 + [vmem] * 3,
        scratch_shapes=[
            pltpu.VMEM((tiles * columns, quantity), jnp.float32),
            dma((len(plan),)),
        ],
        name="unpack_gradients",
    )(whole, therm)


def extended(cells, sides, width):
    for axis, dim in sides:
        count = lax.axis_size(axis)
        head = lax.slice_in_dim(cells, 0, width, axis=dim)
        tail = lax.slice_in_dim(cells, cells.shape[dim] - width, cells.shape[dim], axis=dim)
        cells = jnp.concatenate(
            [
                lax.ppermute(tail, axis, [(i, (i + 1) % count) for i in range(count)]),
                cells,
                lax.ppermute(head, axis, [((i + 1) % count, i) for i in range(count)]),
            ],
            axis=dim,
        )
    return cells


def layer_norm(values, gain):
    centred = values - jnp.mean(values, axis=-1, keepdims=True)
    spread = jnp.mean(centred * centred, axis=-1, keepdims=True)
    return centred * lax.rsqrt(spread + 1e-06) * gain


def regrid(flat_fluxes, cell_ids, margin):
    picked = jnp.take(flat_fluxes, cell_ids, axis=0).astype(jnp.float32)
    factor = margin.astype(jnp.float32)
    weighted = jnp.sum(factor[..., None] * picked, axis=0)
    return (weighted / jnp.sum(factor, axis=0)[..., None]).astype(jnp.bfloat16)


def marine_update_kernel(
    marine_present_latent,
    marine_driver_input,
    latent_adjoint,
    water_indicator_real,
    driver_projection_matrix,
    spatial_kernel_taps,
    layernorm_multiplier,
    pointwise_widen_matrix,
    pointwise_shrink_matrix,
    thermal_projection_matrix,
    haloed_latent,
    haloed_derivative,
):
    horizontal_sum_result, vertical_sum_result, feature_dimension = marine_present_latent.shape
    reach = KS // 2
    forcing_flat = marine_driver_input.reshape(-1, marine_driver_input.shape[-1])
    pushed = jnp.dot(
        forcing_flat, driver_projection_matrix, preferred_element_type=jnp.float32
    ).reshape(horizontal_sum_result, vertical_sum_result, feature_dimension)
    mixed = (marine_present_latent.astype(jnp.float32) + pushed).astype(jnp.bfloat16)
    padded = jnp.pad(haloed_latent(mixed), ((reach, reach), (0, 0), (0, 0))).astype(jnp.float32)
    conv_out = jnp.zeros(
        (horizontal_sum_result, vertical_sum_result, feature_dimension), jnp.float32
    )
    for row_off in range(KS):
        for col_off in range(KS):
            conv_out = (
                conv_out
                + spatial_kernel_taps[row_off * KS + col_off]
                * padded[
                    row_off : row_off + horizontal_sum_result,
                    col_off : col_off + vertical_sum_result,
                ]
            )
    normed_f, pull_norm = jax.vjp(
        layer_norm, conv_out.reshape(-1, feature_dimension), layernorm_multiplier
    )
    normed = normed_f.astype(jnp.bfloat16)
    hidden_pre = jnp.dot(normed, pointwise_widen_matrix, preferred_element_type=jnp.float32)
    hidden_f, pull_gelu = jax.vjp(jax.nn.gelu, hidden_pre)
    hidden = hidden_f.astype(jnp.bfloat16)
    mlp_out = jnp.dot(hidden, pointwise_shrink_matrix, preferred_element_type=jnp.float32)
    sea_column = water_indicator_real.reshape(-1, 1)
    marine_successor_latent = (
        sea_column * (mixed.reshape(-1, feature_dimension).astype(jnp.float32) + mlp_out)
    ).astype(jnp.bfloat16)
    thermal_highres_field = jnp.dot(
        marine_successor_latent, thermal_projection_matrix, preferred_element_type=jnp.float32
    )
    thermal_highres_field = thermal_highres_field.reshape(
        horizontal_sum_result // SUBDIVISION,
        SUBDIVISION,
        vertical_sum_result // SUBDIVISION,
        SUBDIVISION,
        thermal_highres_field.shape[-1],
    )
    marine_site_number = jnp.sum(
        water_indicator_real.reshape(
            horizontal_sum_result // SUBDIVISION,
            SUBDIVISION,
            vertical_sum_result // SUBDIVISION,
            SUBDIVISION,
        ),
        axis=(1, 3),
    )
    thermal_lowres_field = (
        jnp.sum(thermal_highres_field, axis=(1, 3))
        / jnp.maximum(marine_site_number, 1.0)[..., None]
    ).astype(jnp.bfloat16)
    masked_cot = (
        sea_column * latent_adjoint.reshape(-1, feature_dimension).astype(jnp.float32)
    ).astype(jnp.bfloat16)
    grad_down = jnp.dot(hidden.T, masked_cot, preferred_element_type=jnp.float32)
    hidden_cot = jnp.dot(masked_cot, pointwise_shrink_matrix.T, preferred_element_type=jnp.float32)
    pre_cot = pull_gelu(hidden_cot)[0].astype(jnp.bfloat16)
    grad_up = jnp.dot(normed.T, pre_cot, preferred_element_type=jnp.float32)
    normed_cot = jnp.dot(pre_cot, pointwise_widen_matrix.T, preferred_element_type=jnp.float32)
    conv_cot, grad_gain = pull_norm(normed_cot)
    conv_cot = conv_cot.reshape(horizontal_sum_result, vertical_sum_result, feature_dimension)
    tap_grads = []
    for row_off in range(KS):
        for col_off in range(KS):
            tap_grads.append(
                jnp.sum(
                    conv_cot
                    * padded[
                        row_off : row_off + horizontal_sum_result,
                        col_off : col_off + vertical_sum_result,
                    ],
                    axis=(0, 1),
                )
            )
    grad_padded = jnp.pad(haloed_derivative(conv_cot), ((reach, reach), (0, 0), (0, 0)))
    back = masked_cot.astype(jnp.float32).reshape(
        horizontal_sum_result, vertical_sum_result, feature_dimension
    )
    for row_off in range(KS):
        for col_off in range(KS):
            row_from = KS - 1 - row_off
            col_from = KS - 1 - col_off
            back = (
                back
                + spatial_kernel_taps[row_off * KS + col_off]
                * grad_padded[
                    row_from : row_from + horizontal_sum_result,
                    col_from : col_from + vertical_sum_result,
                ]
            )
    marine_latent_adjoint = back.astype(jnp.bfloat16)
    grad_force = jnp.dot(
        forcing_flat.T,
        marine_latent_adjoint.reshape(-1, feature_dimension),
        preferred_element_type=jnp.float32,
    )
    derivative_sequence = (grad_force, jnp.stack(tap_grads), grad_gain, grad_up, grad_down)
    return (
        marine_successor_latent.reshape(
            horizontal_sum_result, vertical_sum_result, feature_dimension
        ),
        thermal_lowres_field,
        marine_latent_adjoint,
        derivative_sequence,
    )


def pad_state_cols(values):
    return extended(values, (("tile", 1),), KS // 2)


def pad_grad_cols(values):
    return extended(values, (("tile", 1),), KS // 2)


def body(
    air_latent_array,
    air_exchange_projection,
    marine_latent_array,
    driver_projection_matrix,
    spatial_kernel_taps,
    layernorm_multiplier,
    pointwise_widen_matrix,
    pointwise_shrink_matrix,
    thermal_projection_matrix,
    intersecting_air_sites,
    margin_multiplier,
    terrain_water_indicator,
    marine_successor_adjoint,
):
    band = air_latent_array[0]
    band_rows, band_cols, atmos_width = band.shape
    fluxes = jnp.dot(
        band.reshape(-1, atmos_width), air_exchange_projection, preferred_element_type=jnp.float32
    ).astype(jnp.bfloat16)
    fluxes = fluxes.reshape(band_rows, band_cols, fluxes.shape[-1])
    strip = lax.all_to_all(fluxes, "tile", split_axis=1, concat_axis=0, tiled=True)
    marine_driver_input = regrid(
        strip.reshape(-1, strip.shape[-1]), intersecting_air_sites, margin_multiplier
    )
    water_indicator_real = terrain_water_indicator.astype(jnp.float32)
    marine_successor_latent, thermal_lowres_field, marine_latent_adjoint, derivative_sequence = (
        marine_update_kernel(
            marine_latent_array[0],
            marine_driver_input,
            marine_successor_adjoint[0],
            water_indicator_real,
            driver_projection_matrix,
            spatial_kernel_taps,
            layernorm_multiplier,
            pointwise_widen_matrix,
            pointwise_shrink_matrix,
            thermal_projection_matrix,
            pad_state_cols,
            pad_grad_cols,
        )
    )
    cell_total = (
        lax.axis_size("ens")
        * lax.axis_size("tile")
        * marine_successor_latent.shape[0]
        * marine_successor_latent.shape[1]
    )
    grad_scale = 1.0 / math.sqrt(cell_total)
    grad_force, grad_conv, grad_gain, grad_up, grad_down = derivative_sequence
    up, down, force, conv, gain, thermal_strip_slice = reduce_gradients(
        grad_up,
        grad_down,
        grad_force,
        grad_conv,
        grad_gain.reshape(1, -1),
        thermal_lowres_field.astype(jnp.float32),
        grad_scale,
    )
    return (
        marine_successor_latent[None],
        thermal_strip_slice[None],
        marine_latent_adjoint[None],
        force,
        conv,
        gain.reshape(-1),
        up,
        down,
    )


def solution(mesh):
    return jax.shard_map(
        body,
        mesh=mesh,
        in_specs=(
            P("ens", "tile", None, None),
            P(),
            P("ens", None, "tile", None),
            P(),
            P(),
            P(),
            P(),
            P(),
            P(),
            P(None, None, "tile"),
            P(None, None, "tile"),
            P(None, "tile"),
            P("ens", None, "tile", None),
        ),
        out_specs=(
            P("ens", None, "tile", None),
            P("ens", "tile", None, None),
            P("ens", None, "tile", None),
            P(),
            P(),
            P(),
            P(),
            P(),
        ),
        check_vma=False,
    )
```

```python
import functools
import math

import jax
import jax.numpy as jnp
from jax import lax
from jax.experimental import pallas as pl
from jax.experimental.pallas import tpu as pltpu
from jax.sharding import PartitionSpec as P

SUBDIVISION = 4
KS = 3
LANES = 128
SLABS = 3
MESH = pl.DeviceIdType.MESH


def pack_plan(shapes):
    plan, at = [], 0
    for which, (rows, cols) in enumerate(shapes):
        for col in range(0, cols, LANES):
            plan.append((which, col, at, rows))
            at += rows
    return plan, at


def reduce_kernel(
    scale,
    ne,
    nt,
    rows,
    plan,
    used,
    up_ref,
    down_ref,
    force_ref,
    conv_ref,
    gain_ref,
    therm_ref,
    whole,
    therm_out,
    small,
    packed,
    from_core,
    halves,
    from_ens,
    part,
    from_z,
    therm_in,
    t_send,
    t_recv,
    a_send,
    a_recv,
    b_send,
    b_recv,
    c_send,
    c_recv,
    d_send,
    d_recv,
    e_send,
    e_recv,
    f_send,
    f_recv,
):
    nz = nt // 2
    block = nz * rows
    slab = 2 * ne * block
    ens = lax.axis_index("ens")
    tile = lax.axis_index("tile")
    z = tile // 2
    core = tile % 2
    other = 1 - core
    mate = {"tile": z * 2 + other}

    def send(src, dst, s_sem, r_sem, device):
        copy = pltpu.make_async_remote_copy(
            src_ref=src,
            dst_ref=dst,
            send_sem=s_sem,
            recv_sem=r_sem,
            device_id=device,
            device_id_type=MESH,
        )
        copy.start()
        return copy

    def at_block(s, h, e):
        return pl.ds(pl.multiple_of(s * slab + (h * ne + e) * block, 16), block)

    def at_chunk(where):
        return pl.ds(pl.multiple_of(where * rows, 16), rows)

    barrier = pltpu.get_barrier_semaphore()
    for o in range(1, nt):
        pl.semaphore_signal(
            barrier, inc=1, device_id={"tile": (tile + o) % nt}, device_id_type=MESH
        )
    for o in range(1, ne):
        pl.semaphore_signal(
            barrier, inc=1, device_id={"ens": (ens + o) % ne}, device_id_type=MESH
        )

    taps = conv_ref.shape[0]
    small[...] = jnp.zeros_like(small)
    small[0:taps, :] = conv_ref[...]
    small[taps : taps + 1, :] = gain_ref[...]
    ins = (up_ref, down_ref, force_ref, small)
    if used < SLABS * slab:
        packed[used : SLABS * slab, :] = jnp.zeros((SLABS * slab - used, LANES), jnp.bfloat16)

    order = list(range(1, ne)) + [0]
    a_copies = [[] for _ in range(SLABS)]

    def send_slab(s):
        for o in order:
            e = (ens + o) % ne
            a_copies[s].append(
                send(
                    packed.at[at_block(s, other, e)],
                    from_core.at[s, o],
                    a_send.at[s, o],
                    a_recv.at[s, o],
                    mate,
                )
            )

    ready = 0
    for which, col, at, count in plan:
        packed[at : at + count, :] = ins[which][:, col : col + LANES].astype(jnp.bfloat16)
        while ready < SLABS and at + count >= min((ready + 1) * slab, used):
            if ready == 0:
                pl.semaphore_wait(barrier, nt - 1 + ne - 1)
            send_slab(ready)
            ready += 1

    t_copies = []
    for o in range(1, nt):
        to = (tile + o) % nt
        t_copies.append(
            send(
                therm_ref.at[to],
                therm_in.at[o],
                t_send.at[o],
                t_recv.at[o],
                {"tile": to},
            )
        )
    b_copies = [[] for _ in range(SLABS)]
    for s in range(SLABS):
        for o, copy in zip(order, a_copies[s]):
            e = (ens + o) % ne
            copy.wait_recv()
            halves[s, o] = (
                packed[at_block(s, core, e), :].astype(jnp.float32)
                + from_core[s, o].astype(jnp.float32)
            ).astype(jnp.bfloat16)
            if o:
                b_copies[s].append(
                    send(
                        halves.at[s, o],
                        from_ens.at[s, o],
                        b_send.at[s, o],
                        b_recv.at[s, o],
                        {"ens": e},
                    )
                )
    c_copies = [[] for _ in range(SLABS)]
    for s in range(SLABS):
        total = halves[s, 0].astype(jnp.float32)
        for o, copy in zip(range(1, ne), b_copies[s]):
            copy.wait_recv()
            total = total + from_ens[s, o].astype(jnp.float32)
        part[s] = total.astype(jnp.bfloat16)
        for o in range(1, nz):
            to = (z + o) % nz
            c_copies[s].append(
                send(
                    part.at[s, at_chunk(to)],
                    from_z.at[s, o],
                    c_send.at[s, o],
                    c_recv.at[s, o],
                    {"tile": to * 2 + core},
                )
            )
    d_copies = [[] for _ in range(SLABS)]
    for s in range(SLABS):
        mine = part[s, at_chunk(z), :].astype(jnp.float32)
        for o, copy in zip(range(1, nz), c_copies[s]):
            copy.wait_recv()
            mine = mine + from_z[s, o].astype(jnp.float32)
        spot = at_chunk(((s * 2 + core) * ne + ens) * nz + z)
        whole[spot, :] = (mine * scale).astype(jnp.bfloat16)
        for o in range(1, nz):
            to = (z + o) % nz
            d_copies[s].append(
                send(
                    whole.at[spot],
                    whole.at[spot],
                    d_send.at[s, o],
                    d_recv.at[s, o],
                    {"tile": to * 2 + core},
                )
            )
    e_copies = [[] for _ in range(SLABS)]
    f_copies = []
    for s in range(SLABS):
        for copy in d_copies[s]:
            copy.wait_recv()
        own = at_block(s, core, ens)
        for o in range(1, ne):
            e_copies[s].append(
                send(
                    whole.at[own],
                    whole.at[own],
                    e_send.at[s, o],
                    e_recv.at[s, o],
                    {"ens": (ens + o) % ne},
                )
            )
        f_copies.append(send(whole.at[own], whole.at[own], f_send.at[s, 0], f_recv.at[s, 0], mate))
    for s in range(SLABS):
        for o, copy in zip(range(1, ne), e_copies[s]):
            copy.wait_recv()
            theirs = at_block(s, core, (ens + ne - o) % ne)
            f_copies.append(
                send(whole.at[theirs], whole.at[theirs], f_send.at[s, o], f_recv.at[s, o], mate)
            )
    therm_out[tile] = therm_ref[tile]
    for o, copy in zip(range(1, nt), t_copies):
        copy.wait_recv()
        therm_out[(tile + nt - o) % nt] = therm_in[o]
    for copy in f_copies:
        copy.wait_recv()
    sent = t_copies + f_copies
    for group in (a_copies, b_copies, c_copies, d_copies, e_copies):
        for copies in group:
            sent = sent + copies
    for copy in sent:
        copy.wait_send()


def unpack_kernel(
    plan, whole, therm, up_out, down_out, force_out, conv_out, gain_out, therm_out, strip, sems
):
    outs = (up_out, down_out, force_out)
    copies = []
    for i, (which, col, at, count) in enumerate(plan):
        if which < len(outs):
            copies.append(
                pltpu.make_async_copy(
                    whole.at[at : at + count, :],
                    outs[which].at[:, col : col + LANES],
                    sems.at[i],
                )
            )
            copies[-1].start()
    taps = conv_out.shape[0]
    for which, col, at, count in plan:
        if which == len(outs):
            rows = whole[at : at + count, :].astype(jnp.float32)
            conv_out[:, col : col + LANES] = rows[:taps].astype(jnp.bfloat16)
            gain_out[:, col : col + LANES] = rows[taps : taps + 1].astype(jnp.bfloat16)
    tiles, columns, _ = therm.shape
    for t in range(tiles):
        strip[t * columns : (t + 1) * columns, :] = therm[t]
    therm_out[0] = strip[...].astype(jnp.bfloat16)
    for copy in copies:
        copy.wait()


def reduce_gradients(up, down, force, conv, gain, therm, scale):
    ne, nt = lax.axis_size("ens"), lax.axis_size("tile")
    nz = nt // 2
    taps, features = conv.shape
    small_rows = -(-(taps + 1) // 16) * 16
    plan, used = pack_plan([up.shape, down.shape, force.shape, (small_rows, features)])
    rows = -(-used // (SLABS * 2 * ne * nz * 16)) * 16
    block = nz * rows
    bf16 = jnp.bfloat16
    dma = pltpu.SemaphoreType.DMA
    vmem = pl.BlockSpec(memory_space=pltpu.VMEM)
    anywhere = pl.BlockSpec(memory_space=pl.ANY)
    tiles, columns, quantity = therm.shape
    whole, therm = pl.pallas_call(
        functools.partial(reduce_kernel, scale, ne, nt, rows, plan, used),
        out_shape=[
            jax.ShapeDtypeStruct((SLABS * 2 * ne * block, LANES), bf16),
            jax.ShapeDtypeStruct(therm.shape, therm.dtype),
        ],
        in_specs=[vmem] * 6,
        out_specs=[vmem] * 2,
        scratch_shapes=[
            pltpu.VMEM((small_rows, features), jnp.float32),
            pltpu.VMEM((SLABS * 2 * ne * block, LANES), bf16),
            pltpu.VMEM((SLABS, ne, block, LANES), bf16),
            pltpu.VMEM((SLABS, ne, block, LANES), bf16),
            pltpu.VMEM((SLABS, ne, block, LANES), bf16),
            pltpu.VMEM((SLABS, block, LANES), bf16),
            pltpu.VMEM((SLABS, nz, rows, LANES), bf16),
            pltpu.VMEM(therm.shape, therm.dtype),
        ]
        + [dma((nt,)), dma((nt,))]
        + [dma((SLABS, ne)), dma((SLABS, ne))] * 2
        + [dma((SLABS, nz)), dma((SLABS, nz))] * 2
        + [dma((SLABS, ne)), dma((SLABS, ne))] * 2,
        compiler_params=pltpu.CompilerParams(collective_id=1, has_side_effects=True),
        name="reduce_gradients",
    )(up, down, force, conv, gain, therm)
    return pl.pallas_call(
        functools.partial(unpack_kernel, plan),
        out_shape=[
            jax.ShapeDtypeStruct(up.shape, bf16),
            jax.ShapeDtypeStruct(down.shape, bf16),
            jax.ShapeDtypeStruct(force.shape, bf16),
            jax.ShapeDtypeStruct(conv.shape, bf16),
            jax.ShapeDtypeStruct(gain.shape, bf16),
            jax.ShapeDtypeStruct((1, tiles * columns, quantity), bf16),
        ],
        in_specs=[vmem] * 2,
        out_specs=[anywhere] * 3 + [vmem] * 3,
        scratch_shapes=[
            pltpu.VMEM((tiles * columns, quantity), jnp.float32),
            dma((len(plan),)),
        ],
        name="unpack_gradients",
    )(whole, therm)


def mix_kernel(
    nt,
    cols,
    air_ref,
    exchange_ref,
    weights_ref,
    latent_ref,
    driver_ref,
    forcing_out,
    mixed_out,
    left_out,
    right_out,
    flux,
    slabs,
    strip_in,
    strip,
    state,
    edges,
    s_send,
    s_recv,
    h_send,
    h_recv,
):
    tile = lax.axis_index("tile")
    bf16, f32 = jnp.bfloat16, jnp.float32
    barrier = pltpu.get_barrier_semaphore()
    for o in range(1, nt):
        pl.semaphore_signal(
            barrier, inc=1, device_id={"tile": (tile + o) % nt}, device_id_type=MESH
        )
    flux[...] = (
        jnp.dot(air_ref[...], exchange_ref[...], preferred_element_type=f32)
        .astype(bf16)
        .astype(f32)
    )
    share = slabs.shape[1]
    for t in range(nt):
        slabs[t] = flux[t * share : (t + 1) * share, :]
    pl.semaphore_wait(barrier, nt - 1)
    copies = []
    for o in range(1, nt):
        to = (tile + o) % nt
        copies.append(
            pltpu.make_async_remote_copy(
                src_ref=slabs.at[to],
                dst_ref=strip_in.at[tile],
                send_sem=s_send.at[o],
                recv_sem=s_recv.at[o],
                device_id={"tile": to},
                device_id_type=MESH,
            )
        )
        copies[-1].start()
    strip_in[tile] = slabs[tile]
    weights = weights_ref[...]
    over_sites = (((0,), (0,)), ((), ()))
    total = lax.dot_general(
        weights,
        jnp.ones((weights.shape[0], strip.shape[1]), bf16),
        over_sites,
        preferred_element_type=f32,
    )
    for copy in copies:
        copy.wait_recv()
    for t in range(nt):
        strip[t * share : (t + 1) * share, :] = strip_in[t]
    weighted = lax.dot_general(
        weights, strip[...].astype(bf16), over_sites, preferred_element_type=f32
    )
    forcing = (weighted / total).astype(bf16)
    forcing_out[...] = forcing
    mixed = (
        latent_ref[...].astype(f32)
        + jnp.dot(forcing, driver_ref[...], preferred_element_type=f32)
    ).astype(bf16)
    for lane in range(0, mixed.shape[1], LANES):
        state[lane // LANES] = mixed[:, lane : lane + LANES].astype(f32)
    rows = edges.shape[1]
    for side, column in ((0, cols - 1), (1, 0)):
        for lane in range(0, mixed.shape[1], LANES):
            edges[side, :, lane : lane + LANES] = state[
                lane // LANES, pl.ds(column, rows, stride=cols), :
            ].astype(bf16)
    hops = ((0, left_out, (tile + 1) % nt), (1, right_out, (tile + nt - 1) % nt))
    halos = []
    for side, out, to in hops:
        halos.append(
            pltpu.make_async_remote_copy(
                src_ref=edges.at[side],
                dst_ref=out,
                send_sem=h_send.at[side],
                recv_sem=h_recv.at[side],
                device_id={"tile": to},
                device_id_type=MESH,
            )
        )
        halos[-1].start()
    mixed_out[...] = mixed
    for copy in halos:
        copy.wait_recv()
    for copy in copies + halos:
        copy.wait_send()


def mix_states(band, exchange, sites, margin, latent, driver):
    nt = lax.axis_size("tile")
    rows, cols, features = latent.shape
    quantity = exchange.shape[1]
    places = band.shape[0]
    cells = rows * cols
    flat_sites = sites.reshape(sites.shape[0], 1, cells)
    flat_margin = margin.reshape(margin.shape[0], 1, cells)
    names = lax.broadcasted_iota(jnp.int32, (1, places, 1), 1)
    weights = jnp.sum(jnp.where(flat_sites == names, flat_margin, 0), axis=0)
    bf16, f32 = jnp.bfloat16, jnp.float32
    dma = pltpu.SemaphoreType.DMA
    vmem = pl.BlockSpec(memory_space=pltpu.VMEM)
    return pl.pallas_call(
        functools.partial(mix_kernel, nt, cols),
        out_shape=[
            jax.ShapeDtypeStruct((cells, quantity), bf16),
            jax.ShapeDtypeStruct((cells, features), bf16),
            jax.ShapeDtypeStruct((rows, features), bf16),
            jax.ShapeDtypeStruct((rows, features), bf16),
        ],
        in_specs=[vmem] * 5,
        out_specs=[vmem] * 4,
        scratch_shapes=[
            pltpu.VMEM((places, quantity), f32),
            pltpu.VMEM((nt, places // nt, quantity), f32),
            pltpu.VMEM((nt, places // nt, quantity), f32),
            pltpu.VMEM((places, quantity), f32),
            pltpu.VMEM((features // LANES, cells, LANES), f32),
            pltpu.VMEM((2, rows, features), bf16),
            dma((nt,)),
            dma((nt,)),
            dma((2,)),
            dma((2,)),
        ],
        compiler_params=pltpu.CompilerParams(collective_id=2, has_side_effects=True),
        name="mix_states",
    )(band, exchange, weights.astype(bf16), latent.reshape(cells, features), driver)


def extended(cells, sides, width):
    for axis, dim in sides:
        count = lax.axis_size(axis)
        head = lax.slice_in_dim(cells, 0, width, axis=dim)
        tail = lax.slice_in_dim(cells, cells.shape[dim] - width, cells.shape[dim], axis=dim)
        cells = jnp.concatenate(
            [
                lax.ppermute(tail, axis, [(i, (i + 1) % count) for i in range(count)]),
                cells,
                lax.ppermute(head, axis, [((i + 1) % count, i) for i in range(count)]),
            ],
            axis=dim,
        )
    return cells


def layer_norm(values, gain):
    centred = values - jnp.mean(values, axis=-1, keepdims=True)
    spread = jnp.mean(centred * centred, axis=-1, keepdims=True)
    return centred * lax.rsqrt(spread + 1e-06) * gain


def marine_update_kernel(
    marine_present_latent,
    marine_driver_input,
    latent_adjoint,
    water_indicator_real,
    driver_projection_matrix,
    spatial_kernel_taps,
    layernorm_multiplier,
    pointwise_widen_matrix,
    pointwise_shrink_matrix,
    thermal_projection_matrix,
    haloed_derivative,
):
    horizontal_sum_result, vertical_sum_result, feature_dimension = marine_present_latent.shape
    reach = KS // 2
    forcing_flat, mixed, left, right = marine_driver_input
    mixed = mixed.reshape(horizontal_sum_result, vertical_sum_result, feature_dimension)
    haloed = jnp.concatenate([left[:, None], mixed, right[:, None]], axis=1)
    padded = jnp.pad(haloed, ((reach, reach), (0, 0), (0, 0))).astype(jnp.float32)
    conv_out = jnp.zeros(
        (horizontal_sum_result, vertical_sum_result, feature_dimension), jnp.float32
    )
    for row_off in range(KS):
        for col_off in range(KS):
            conv_out = (
                conv_out
                + spatial_kernel_taps[row_off * KS + col_off]
                * padded[
                    row_off : row_off + horizontal_sum_result,
                    col_off : col_off + vertical_sum_result,
                ]
            )
    normed_f, pull_norm = jax.vjp(
        layer_norm, conv_out.reshape(-1, feature_dimension), layernorm_multiplier
    )
    normed = normed_f.astype(jnp.bfloat16)
    hidden_pre = jnp.dot(normed, pointwise_widen_matrix, preferred_element_type=jnp.float32)
    hidden_f, pull_gelu = jax.vjp(jax.nn.gelu, hidden_pre)
    hidden = hidden_f.astype(jnp.bfloat16)
    mlp_out = jnp.dot(hidden, pointwise_shrink_matrix, preferred_element_type=jnp.float32)
    sea_column = water_indicator_real.reshape(-1, 1)
    marine_successor_latent = (
        sea_column * (mixed.reshape(-1, feature_dimension).astype(jnp.float32) + mlp_out)
    ).astype(jnp.bfloat16)
    thermal_highres_field = jnp.dot(
        marine_successor_latent, thermal_projection_matrix, preferred_element_type=jnp.float32
    )
    thermal_highres_field = thermal_highres_field.reshape(
        horizontal_sum_result // SUBDIVISION,
        SUBDIVISION,
        vertical_sum_result // SUBDIVISION,
        SUBDIVISION,
        thermal_highres_field.shape[-1],
    )
    marine_site_number = jnp.sum(
        water_indicator_real.reshape(
            horizontal_sum_result // SUBDIVISION,
            SUBDIVISION,
            vertical_sum_result // SUBDIVISION,
            SUBDIVISION,
        ),
        axis=(1, 3),
    )
    thermal_lowres_field = (
        jnp.sum(thermal_highres_field, axis=(1, 3))
        / jnp.maximum(marine_site_number, 1.0)[..., None]
    ).astype(jnp.bfloat16)
    masked_cot = (
        sea_column * latent_adjoint.reshape(-1, feature_dimension).astype(jnp.float32)
    ).astype(jnp.bfloat16)
    grad_down = jnp.dot(hidden.T, masked_cot, preferred_element_type=jnp.float32)
    hidden_cot = jnp.dot(masked_cot, pointwise_shrink_matrix.T, preferred_element_type=jnp.float32)
    pre_cot = pull_gelu(hidden_cot)[0].astype(jnp.bfloat16)
    grad_up = jnp.dot(normed.T, pre_cot, preferred_element_type=jnp.float32)
    normed_cot = jnp.dot(pre_cot, pointwise_widen_matrix.T, preferred_element_type=jnp.float32)
    conv_cot, grad_gain = pull_norm(normed_cot)
    conv_cot = conv_cot.reshape(horizontal_sum_result, vertical_sum_result, feature_dimension)
    tap_grads = []
    for row_off in range(KS):
        for col_off in range(KS):
            tap_grads.append(
                jnp.sum(
                    conv_cot
                    * padded[
                        row_off : row_off + horizontal_sum_result,
                        col_off : col_off + vertical_sum_result,
                    ],
                    axis=(0, 1),
                )
            )
    grad_padded = jnp.pad(haloed_derivative(conv_cot), ((reach, reach), (0, 0), (0, 0)))
    back = masked_cot.astype(jnp.float32).reshape(
        horizontal_sum_result, vertical_sum_result, feature_dimension
    )
    for row_off in range(KS):
        for col_off in range(KS):
            row_from = KS - 1 - row_off
            col_from = KS - 1 - col_off
            back = (
                back
                + spatial_kernel_taps[row_off * KS + col_off]
                * grad_padded[
                    row_from : row_from + horizontal_sum_result,
                    col_from : col_from + vertical_sum_result,
                ]
            )
    marine_latent_adjoint = back.astype(jnp.bfloat16)
    grad_force = jnp.dot(
        forcing_flat.T,
        marine_latent_adjoint.reshape(-1, feature_dimension),
        preferred_element_type=jnp.float32,
    )
    derivative_sequence = (grad_force, jnp.stack(tap_grads), grad_gain, grad_up, grad_down)
    return (
        marine_successor_latent.reshape(
            horizontal_sum_result, vertical_sum_result, feature_dimension
        ),
        thermal_lowres_field,
        marine_latent_adjoint,
        derivative_sequence,
    )


def pad_grad_cols(values):
    return extended(values, (("tile", 1),), KS // 2)


def body(
    air_latent_array,
    air_exchange_projection,
    marine_latent_array,
    driver_projection_matrix,
    spatial_kernel_taps,
    layernorm_multiplier,
    pointwise_widen_matrix,
    pointwise_shrink_matrix,
    thermal_projection_matrix,
    intersecting_air_sites,
    margin_multiplier,
    terrain_water_indicator,
    marine_successor_adjoint,
):
    band = air_latent_array[0]
    band_rows, band_cols, atmos_width = band.shape
    marine_driver_input = mix_states(
        band.reshape(-1, atmos_width),
        air_exchange_projection,
        intersecting_air_sites,
        margin_multiplier,
        marine_latent_array[0],
        driver_projection_matrix,
    )
    water_indicator_real = terrain_water_indicator.astype(jnp.float32)
    marine_successor_latent, thermal_lowres_field, marine_latent_adjoint, derivative_sequence = (
        marine_update_kernel(
            marine_latent_array[0],
            marine_driver_input,
            marine_successor_adjoint[0],
            water_indicator_real,
            driver_projection_matrix,
            spatial_kernel_taps,
            layernorm_multiplier,
            pointwise_widen_matrix,
            pointwise_shrink_matrix,
            thermal_projection_matrix,
            pad_grad_cols,
        )
    )
    cell_total = (
        lax.axis_size("ens")
        * lax.axis_size("tile")
        * marine_successor_latent.shape[0]
        * marine_successor_latent.shape[1]
    )
    grad_scale = 1.0 / math.sqrt(cell_total)
    grad_force, grad_conv, grad_gain, grad_up, grad_down = derivative_sequence
    up, down, force, conv, gain, thermal_strip_slice = reduce_gradients(
        grad_up,
        grad_down,
        grad_force,
        grad_conv,
        grad_gain.reshape(1, -1),
        thermal_lowres_field.astype(jnp.float32),
        grad_scale,
    )
    return (
        marine_successor_latent[None],
        thermal_strip_slice[None],
        marine_latent_adjoint[None],
        force,
        conv,
        gain.reshape(-1),
        up,
        down,
    )


def solution(mesh):
    return jax.shard_map(
        body,
        mesh=mesh,
        in_specs=(
            P("ens", "tile", None, None),
            P(),
            P("ens", None, "tile", None),
            P(),
            P(),
            P(),
            P(),
            P(),
            P(),
            P(None, None, "tile"),
            P(None, None, "tile"),
            P(None, "tile"),
            P("ens", None, "tile", None),
        ),
        out_specs=(
            P("ens", None, "tile", None),
            P("ens", "tile", None, None),
            P("ens", None, "tile", None),
            P(),
            P(),
            P(),
            P(),
            P(),
        ),
        check_vma=False,
    )
```

```python
import functools
import math

import jax
import jax.numpy as jnp
from jax import lax
from jax.experimental import pallas as pl
from jax.experimental.pallas import tpu as pltpu
from jax.sharding import PartitionSpec as P

SUBDIVISION = 4
KS = 3
LANES = 128
SLABS = 3
MESH = pl.DeviceIdType.MESH


def pack_plan(shapes):
    plan, at = [], 0
    for which, (rows, cols) in enumerate(shapes):
        for col in range(0, cols, LANES):
            plan.append((which, col, at, rows))
            at += rows
    return plan, at


def reduce_kernel(
    scale,
    ne,
    nt,
    rows,
    plan,
    used,
    up_ref,
    down_ref,
    force_ref,
    conv_ref,
    gain_ref,
    therm_ref,
    whole,
    therm_out,
    small,
    packed,
    from_core,
    halves,
    from_ens,
    part,
    from_z,
    therm_in,
    t_send,
    t_recv,
    a_send,
    a_recv,
    b_send,
    b_recv,
    c_send,
    c_recv,
    d_send,
    d_recv,
    e_send,
    e_recv,
    f_send,
    f_recv,
):
    nz = nt // 2
    block = nz * rows
    slab = 2 * ne * block
    ens = lax.axis_index("ens")
    tile = lax.axis_index("tile")
    z = tile // 2
    core = tile % 2
    other = 1 - core
    mate = {"tile": z * 2 + other}

    def send(src, dst, s_sem, r_sem, device):
        copy = pltpu.make_async_remote_copy(
            src_ref=src,
            dst_ref=dst,
            send_sem=s_sem,
            recv_sem=r_sem,
            device_id=device,
            device_id_type=MESH,
        )
        copy.start()
        return copy

    def at_block(s, h, e):
        return pl.ds(pl.multiple_of(s * slab + (h * ne + e) * block, 16), block)

    def at_chunk(where):
        return pl.ds(pl.multiple_of(where * rows, 16), rows)

    barrier = pltpu.get_barrier_semaphore()
    for o in range(1, nt):
        pl.semaphore_signal(
            barrier, inc=1, device_id={"tile": (tile + o) % nt}, device_id_type=MESH
        )
    for o in range(1, ne):
        pl.semaphore_signal(
            barrier, inc=1, device_id={"ens": (ens + o) % ne}, device_id_type=MESH
        )

    taps = conv_ref.shape[0]
    small[...] = jnp.zeros_like(small)
    small[0:taps, :] = conv_ref[...]
    small[taps : taps + 1, :] = gain_ref[...]
    ins = (up_ref, down_ref, force_ref, small)
    if used < SLABS * slab:
        packed[used : SLABS * slab, :] = jnp.zeros((SLABS * slab - used, LANES), jnp.bfloat16)

    order = list(range(1, ne)) + [0]
    a_copies = [[] for _ in range(SLABS)]

    def send_slab(s):
        for o in order:
            e = (ens + o) % ne
            a_copies[s].append(
                send(
                    packed.at[at_block(s, other, e)],
                    from_core.at[s, o],
                    a_send.at[s, o],
                    a_recv.at[s, o],
                    mate,
                )
            )

    ready = 0
    for which, col, at, count in plan:
        packed[at : at + count, :] = ins[which][:, col : col + LANES].astype(jnp.bfloat16)
        while ready < SLABS and at + count >= min((ready + 1) * slab, used):
            if ready == 0:
                pl.semaphore_wait(barrier, nt - 1 + ne - 1)
            send_slab(ready)
            ready += 1

    t_copies = []
    for o in range(1, nt):
        to = (tile + o) % nt
        t_copies.append(
            send(
                therm_ref.at[to],
                therm_in.at[o],
                t_send.at[o],
                t_recv.at[o],
                {"tile": to},
            )
        )
    b_copies = [[] for _ in range(SLABS)]
    for s in range(SLABS):
        for o, copy in zip(order, a_copies[s]):
            e = (ens + o) % ne
            copy.wait_recv()
            halves[s, o] = (
                packed[at_block(s, core, e), :].astype(jnp.float32)
                + from_core[s, o].astype(jnp.float32)
            ).astype(jnp.bfloat16)
            if o:
                b_copies[s].append(
                    send(
                        halves.at[s, o],
                        from_ens.at[s, o],
                        b_send.at[s, o],
                        b_recv.at[s, o],
                        {"ens": e},
                    )
                )
    c_copies = [[] for _ in range(SLABS)]
    for s in range(SLABS):
        total = halves[s, 0].astype(jnp.float32)
        for o, copy in zip(range(1, ne), b_copies[s]):
            copy.wait_recv()
            total = total + from_ens[s, o].astype(jnp.float32)
        part[s] = total.astype(jnp.bfloat16)
        for o in range(1, nz):
            to = (z + o) % nz
            c_copies[s].append(
                send(
                    part.at[s, at_chunk(to)],
                    from_z.at[s, o],
                    c_send.at[s, o],
                    c_recv.at[s, o],
                    {"tile": to * 2 + core},
                )
            )
    d_copies = [[] for _ in range(SLABS)]
    for s in range(SLABS):
        mine = part[s, at_chunk(z), :].astype(jnp.float32)
        for o, copy in zip(range(1, nz), c_copies[s]):
            copy.wait_recv()
            mine = mine + from_z[s, o].astype(jnp.float32)
        spot = at_chunk(((s * 2 + core) * ne + ens) * nz + z)
        whole[spot, :] = (mine * scale).astype(jnp.bfloat16)
        for o in range(1, nz):
            to = (z + o) % nz
            d_copies[s].append(
                send(
                    whole.at[spot],
                    whole.at[spot],
                    d_send.at[s, o],
                    d_recv.at[s, o],
                    {"tile": to * 2 + core},
                )
            )
    e_copies = [[] for _ in range(SLABS)]
    f_copies = []
    for s in range(SLABS):
        for copy in d_copies[s]:
            copy.wait_recv()
        own = at_block(s, core, ens)
        for o in range(1, ne):
            e_copies[s].append(
                send(
                    whole.at[own],
                    whole.at[own],
                    e_send.at[s, o],
                    e_recv.at[s, o],
                    {"ens": (ens + o) % ne},
                )
            )
        f_copies.append(send(whole.at[own], whole.at[own], f_send.at[s, 0], f_recv.at[s, 0], mate))
    for s in range(SLABS):
        for o, copy in zip(range(1, ne), e_copies[s]):
            copy.wait_recv()
            theirs = at_block(s, core, (ens + ne - o) % ne)
            f_copies.append(
                send(whole.at[theirs], whole.at[theirs], f_send.at[s, o], f_recv.at[s, o], mate)
            )
    therm_out[tile] = therm_ref[tile]
    for o, copy in zip(range(1, nt), t_copies):
        copy.wait_recv()
        therm_out[(tile + nt - o) % nt] = therm_in[o]
    for copy in f_copies:
        copy.wait_recv()
    sent = t_copies + f_copies
    for group in (a_copies, b_copies, c_copies, d_copies, e_copies):
        for copies in group:
            sent = sent + copies
    for copy in sent:
        copy.wait_send()


def unpack_kernel(
    plan, whole, therm, up_out, down_out, force_out, conv_out, gain_out, therm_out, strip, sems
):
    outs = (up_out, down_out, force_out)
    copies = []
    for i, (which, col, at, count) in enumerate(plan):
        if which < len(outs):
            copies.append(
                pltpu.make_async_copy(
                    whole.at[at : at + count, :],
                    outs[which].at[:, col : col + LANES],
                    sems.at[i],
                )
            )
            copies[-1].start()
    taps = conv_out.shape[0]
    for which, col, at, count in plan:
        if which == len(outs):
            rows = whole[at : at + count, :].astype(jnp.float32)
            conv_out[:, col : col + LANES] = rows[:taps].astype(jnp.bfloat16)
            gain_out[col : col + LANES] = rows[taps].astype(jnp.bfloat16)
    tiles, columns, _ = therm.shape
    for t in range(tiles):
        strip[t * columns : (t + 1) * columns, :] = therm[t]
    therm_out[0] = strip[...].astype(jnp.bfloat16)
    for copy in copies:
        copy.wait()


def reduce_gradients(up, down, force, conv, gain, therm, scale):
    ne, nt = lax.axis_size("ens"), lax.axis_size("tile")
    nz = nt // 2
    taps, features = conv.shape
    small_rows = -(-(taps + 1) // 16) * 16
    plan, used = pack_plan([up.shape, down.shape, force.shape, (small_rows, features)])
    rows = -(-used // (SLABS * 2 * ne * nz * 16)) * 16
    block = nz * rows
    bf16 = jnp.bfloat16
    dma = pltpu.SemaphoreType.DMA
    vmem = pl.BlockSpec(memory_space=pltpu.VMEM)
    anywhere = pl.BlockSpec(memory_space=pl.ANY)
    tiles, columns, quantity = therm.shape
    whole, therm = pl.pallas_call(
        functools.partial(reduce_kernel, scale, ne, nt, rows, plan, used),
        out_shape=[
            jax.ShapeDtypeStruct((SLABS * 2 * ne * block, LANES), bf16),
            jax.ShapeDtypeStruct(therm.shape, therm.dtype),
        ],
        in_specs=[vmem] * 6,
        out_specs=[vmem] * 2,
        scratch_shapes=[
            pltpu.VMEM((small_rows, features), jnp.float32),
            pltpu.VMEM((SLABS * 2 * ne * block, LANES), bf16),
            pltpu.VMEM((SLABS, ne, block, LANES), bf16),
            pltpu.VMEM((SLABS, ne, block, LANES), bf16),
            pltpu.VMEM((SLABS, ne, block, LANES), bf16),
            pltpu.VMEM((SLABS, block, LANES), bf16),
            pltpu.VMEM((SLABS, nz, rows, LANES), bf16),
            pltpu.VMEM(therm.shape, therm.dtype),
        ]
        + [dma((nt,)), dma((nt,))]
        + [dma((SLABS, ne)), dma((SLABS, ne))] * 2
        + [dma((SLABS, nz)), dma((SLABS, nz))] * 2
        + [dma((SLABS, ne)), dma((SLABS, ne))] * 2,
        compiler_params=pltpu.CompilerParams(collective_id=1, has_side_effects=True),
        name="reduce_gradients",
    )(up, down, force, conv, gain, therm)
    return pl.pallas_call(
        functools.partial(unpack_kernel, plan),
        out_shape=[
            jax.ShapeDtypeStruct(up.shape, bf16),
            jax.ShapeDtypeStruct(down.shape, bf16),
            jax.ShapeDtypeStruct(force.shape, bf16),
            jax.ShapeDtypeStruct(conv.shape, bf16),
            jax.ShapeDtypeStruct((features,), bf16),
            jax.ShapeDtypeStruct((1, tiles * columns, quantity), bf16),
        ],
        in_specs=[vmem] * 2,
        out_specs=[anywhere] * 3 + [vmem] * 3,
        scratch_shapes=[
            pltpu.VMEM((tiles * columns, quantity), jnp.float32),
            dma((len(plan),)),
        ],
        name="unpack_gradients",
    )(whole, therm)


def mix_kernel(
    nt,
    cols,
    air_ref,
    exchange_ref,
    weights_ref,
    latent_ref,
    driver_ref,
    forcing_out,
    mixed_out,
    padded,
    flux,
    slabs,
    strip_in,
    strip,
    edges,
    halo,
    s_send,
    s_recv,
    h_send,
    h_recv,
):
    tile = lax.axis_index("tile")
    bf16, f32 = jnp.bfloat16, jnp.float32
    barrier = pltpu.get_barrier_semaphore()
    for o in range(1, nt):
        pl.semaphore_signal(
            barrier, inc=1, device_id={"tile": (tile + o) % nt}, device_id_type=MESH
        )
    flux[...] = (
        jnp.dot(air_ref[...], exchange_ref[...], preferred_element_type=f32)
        .astype(bf16)
        .astype(f32)
    )
    share = slabs.shape[1]
    for t in range(nt):
        slabs[t] = flux[t * share : (t + 1) * share, :]
    pl.semaphore_wait(barrier, nt - 1)
    copies = []
    for o in range(1, nt):
        to = (tile + o) % nt
        copies.append(
            pltpu.make_async_remote_copy(
                src_ref=slabs.at[to],
                dst_ref=strip_in.at[tile],
                send_sem=s_send.at[o],
                recv_sem=s_recv.at[o],
                device_id={"tile": to},
                device_id_type=MESH,
            )
        )
        copies[-1].start()
    strip_in[tile] = slabs[tile]
    weights = weights_ref[...]
    over_sites = (((0,), (0,)), ((), ()))
    total = lax.dot_general(
        weights,
        jnp.ones((weights.shape[0], strip.shape[1]), bf16),
        over_sites,
        preferred_element_type=f32,
    )
    for copy in copies:
        copy.wait_recv()
    for t in range(nt):
        strip[t * share : (t + 1) * share, :] = strip_in[t]
    weighted = lax.dot_general(
        weights, strip[...].astype(bf16), over_sites, preferred_element_type=f32
    )
    forcing = (weighted / total).astype(bf16)
    forcing_out[...] = forcing
    mixed = (
        latent_ref[...].astype(f32)
        + jnp.dot(forcing, driver_ref[...], preferred_element_type=f32)
    ).astype(bf16)
    cube = mixed.astype(f32).reshape(edges.shape[1], cols, mixed.shape[1])
    edges[0] = cube[:, cols - 1 : cols, :]
    edges[1] = cube[:, 0:1, :]
    hops = ((0, (tile + 1) % nt), (1, (tile + nt - 1) % nt))
    halos = []
    for side, to in hops:
        halos.append(
            pltpu.make_async_remote_copy(
                src_ref=edges.at[side],
                dst_ref=halo.at[side],
                send_sem=h_send.at[side],
                recv_sem=h_recv.at[side],
                device_id={"tile": to},
                device_id_type=MESH,
            )
        )
        halos[-1].start()
    mixed_out[...] = mixed
    rows = edges.shape[1]
    padded[0] = jnp.zeros_like(padded[0])
    padded[rows + 1] = jnp.zeros_like(padded[0])
    padded[1 : rows + 1, 1 : cols + 1, :] = cube
    for copy in halos:
        copy.wait_recv()
    padded[1 : rows + 1, 0:1, :] = halo[0]
    padded[1 : rows + 1, cols + 1 : cols + 2, :] = halo[1]
    for copy in copies + halos:
        copy.wait_send()


def mix_states(band, exchange, sites, margin, latent, driver):
    nt = lax.axis_size("tile")
    rows, cols, features = latent.shape
    quantity = exchange.shape[1]
    places = band.shape[0]
    cells = rows * cols
    both = (margin * places + sites).reshape(sites.shape[0], 1, cells)
    flat_sites, flat_margin = both % places, both // places
    names = lax.broadcasted_iota(jnp.int32, (1, places, 1), 1)
    weights = jnp.sum(jnp.where(flat_sites == names, flat_margin, 0), axis=0)
    bf16, f32 = jnp.bfloat16, jnp.float32
    dma = pltpu.SemaphoreType.DMA
    vmem = pl.BlockSpec(memory_space=pltpu.VMEM)
    return pl.pallas_call(
        functools.partial(mix_kernel, nt, cols),
        out_shape=[
            jax.ShapeDtypeStruct((cells, quantity), bf16),
            jax.ShapeDtypeStruct((cells, features), bf16),
            jax.ShapeDtypeStruct((rows + 2, cols + 2, features), f32),
        ],
        in_specs=[vmem] * 5,
        out_specs=[vmem] * 3,
        scratch_shapes=[
            pltpu.VMEM((places, quantity), f32),
            pltpu.VMEM((nt, places // nt, quantity), f32),
            pltpu.VMEM((nt, places // nt, quantity), f32),
            pltpu.VMEM((places, quantity), f32),
            pltpu.VMEM((2, rows, 1, features), f32),
            pltpu.VMEM((2, rows, 1, features), f32),
            dma((nt,)),
            dma((nt,)),
            dma((2,)),
            dma((2,)),
        ],
        compiler_params=pltpu.CompilerParams(collective_id=2, has_side_effects=True),
        name="mix_states",
    )(band, exchange, weights.astype(bf16), latent.reshape(cells, features), driver)


def extended(cells, sides, width):
    for axis, dim in sides:
        count = lax.axis_size(axis)
        head = lax.slice_in_dim(cells, 0, width, axis=dim)
        tail = lax.slice_in_dim(cells, cells.shape[dim] - width, cells.shape[dim], axis=dim)
        cells = jnp.concatenate(
            [
                lax.ppermute(tail, axis, [(i, (i + 1) % count) for i in range(count)]),
                cells,
                lax.ppermute(head, axis, [((i + 1) % count, i) for i in range(count)]),
            ],
            axis=dim,
        )
    return cells


def layer_norm(values, gain):
    centred = values - jnp.mean(values, axis=-1, keepdims=True)
    spread = jnp.mean(centred * centred, axis=-1, keepdims=True)
    return centred * lax.rsqrt(spread + 1e-06) * gain


def marine_update_kernel(
    marine_present_latent,
    marine_driver_input,
    latent_adjoint,
    water_indicator_real,
    driver_projection_matrix,
    spatial_kernel_taps,
    layernorm_multiplier,
    pointwise_widen_matrix,
    pointwise_shrink_matrix,
    thermal_projection_matrix,
    haloed_derivative,
):
    horizontal_sum_result, vertical_sum_result, feature_dimension = marine_present_latent.shape
    reach = KS // 2
    forcing_flat, mixed, padded = marine_driver_input
    mixed = mixed.reshape(horizontal_sum_result, vertical_sum_result, feature_dimension)
    conv_out = jnp.zeros(
        (horizontal_sum_result, vertical_sum_result, feature_dimension), jnp.float32
    )
    for row_off in range(KS):
        for col_off in range(KS):
            conv_out = (
                conv_out
                + spatial_kernel_taps[row_off * KS + col_off]
                * padded[
                    row_off : row_off + horizontal_sum_result,
                    col_off : col_off + vertical_sum_result,
                ]
            )
    normed_f, pull_norm = jax.vjp(
        layer_norm, conv_out.reshape(-1, feature_dimension), layernorm_multiplier
    )
    normed = normed_f.astype(jnp.bfloat16)
    hidden_pre = jnp.dot(normed, pointwise_widen_matrix, preferred_element_type=jnp.float32)
    hidden_f, pull_gelu = jax.vjp(jax.nn.gelu, hidden_pre)
    hidden = hidden_f.astype(jnp.bfloat16)
    mlp_out = jnp.dot(hidden, pointwise_shrink_matrix, preferred_element_type=jnp.float32)
    sea_column = water_indicator_real.reshape(-1, 1)
    marine_successor_latent = (
        sea_column * (mixed.reshape(-1, feature_dimension).astype(jnp.float32) + mlp_out)
    ).astype(jnp.bfloat16)
    thermal_highres_field = jnp.dot(
        marine_successor_latent, thermal_projection_matrix, preferred_element_type=jnp.float32
    )
    thermal_highres_field = thermal_highres_field.reshape(
        horizontal_sum_result // SUBDIVISION,
        SUBDIVISION,
        vertical_sum_result // SUBDIVISION,
        SUBDIVISION,
        thermal_highres_field.shape[-1],
    )
    marine_site_number = jnp.sum(
        water_indicator_real.reshape(
            horizontal_sum_result // SUBDIVISION,
            SUBDIVISION,
            vertical_sum_result // SUBDIVISION,
            SUBDIVISION,
        ),
        axis=(1, 3),
    )
    thermal_lowres_field = (
        jnp.sum(thermal_highres_field, axis=(1, 3))
        / jnp.maximum(marine_site_number, 1.0)[..., None]
    ).astype(jnp.bfloat16)
    masked_cot = (
        sea_column * latent_adjoint.reshape(-1, feature_dimension).astype(jnp.float32)
    ).astype(jnp.bfloat16)
    grad_down = jnp.dot(hidden.T, masked_cot, preferred_element_type=jnp.float32)
    hidden_cot = jnp.dot(masked_cot, pointwise_shrink_matrix.T, preferred_element_type=jnp.float32)
    pre_cot = pull_gelu(hidden_cot)[0].astype(jnp.bfloat16)
    grad_up = jnp.dot(normed.T, pre_cot, preferred_element_type=jnp.float32)
    normed_cot = jnp.dot(pre_cot, pointwise_widen_matrix.T, preferred_element_type=jnp.float32)
    conv_cot, grad_gain = pull_norm(normed_cot)
    conv_cot = conv_cot.reshape(horizontal_sum_result, vertical_sum_result, feature_dimension)
    tap_grads = []
    for row_off in range(KS):
        for col_off in range(KS):
            tap_grads.append(
                jnp.sum(
                    conv_cot
                    * padded[
                        row_off : row_off + horizontal_sum_result,
                        col_off : col_off + vertical_sum_result,
                    ],
                    axis=(0, 1),
                )
            )
    grad_padded = jnp.pad(haloed_derivative(conv_cot), ((reach, reach), (0, 0), (0, 0)))
    back = masked_cot.astype(jnp.float32).reshape(
        horizontal_sum_result, vertical_sum_result, feature_dimension
    )
    for row_off in range(KS):
        for col_off in range(KS):
            row_from = KS - 1 - row_off
            col_from = KS - 1 - col_off
            back = (
                back
                + spatial_kernel_taps[row_off * KS + col_off]
                * grad_padded[
                    row_from : row_from + horizontal_sum_result,
                    col_from : col_from + vertical_sum_result,
                ]
            )
    marine_latent_adjoint = back.astype(jnp.bfloat16)
    grad_force = jnp.dot(
        forcing_flat.T,
        marine_latent_adjoint.reshape(-1, feature_dimension),
        preferred_element_type=jnp.float32,
    )
    derivative_sequence = (grad_force, jnp.stack(tap_grads), grad_gain, grad_up, grad_down)
    return (
        marine_successor_latent.reshape(
            horizontal_sum_result, vertical_sum_result, feature_dimension
        ),
        thermal_lowres_field,
        marine_latent_adjoint,
        derivative_sequence,
    )


def pad_grad_cols(values):
    return extended(values, (("tile", 1),), KS // 2)


def body(
    air_latent_array,
    air_exchange_projection,
    marine_latent_array,
    driver_projection_matrix,
    spatial_kernel_taps,
    layernorm_multiplier,
    pointwise_widen_matrix,
    pointwise_shrink_matrix,
    thermal_projection_matrix,
    intersecting_air_sites,
    margin_multiplier,
    terrain_water_indicator,
    marine_successor_adjoint,
):
    band = air_latent_array[0]
    band_rows, band_cols, atmos_width = band.shape
    marine_driver_input = mix_states(
        band.reshape(-1, atmos_width),
        air_exchange_projection,
        intersecting_air_sites,
        margin_multiplier,
        marine_latent_array[0],
        driver_projection_matrix,
    )
    water_indicator_real = terrain_water_indicator.astype(jnp.float32)
    marine_successor_latent, thermal_lowres_field, marine_latent_adjoint, derivative_sequence = (
        marine_update_kernel(
            marine_latent_array[0],
            marine_driver_input,
            marine_successor_adjoint[0],
            water_indicator_real,
            driver_projection_matrix,
            spatial_kernel_taps,
            layernorm_multiplier,
            pointwise_widen_matrix,
            pointwise_shrink_matrix,
            thermal_projection_matrix,
            pad_grad_cols,
        )
    )
    cell_total = (
        lax.axis_size("ens")
        * lax.axis_size("tile")
        * marine_successor_latent.shape[0]
        * marine_successor_latent.shape[1]
    )
    grad_scale = 1.0 / math.sqrt(cell_total)
    grad_force, grad_conv, grad_gain, grad_up, grad_down = derivative_sequence
    up, down, force, conv, gain, thermal_strip_slice = reduce_gradients(
        grad_up,
        grad_down,
        grad_force,
        grad_conv,
        grad_gain.reshape(1, -1),
        thermal_lowres_field.astype(jnp.float32),
        grad_scale,
    )
    return (
        marine_successor_latent[None],
        thermal_strip_slice[None],
        marine_latent_adjoint[None],
        force,
        conv,
        gain,
        up,
        down,
    )


def solution(mesh):
    return jax.shard_map(
        body,
        mesh=mesh,
        in_specs=(
            P("ens", "tile", None, None),
            P(),
            P("ens", None, "tile", None),
            P(),
            P(),
            P(),
            P(),
            P(),
            P(),
            P(None, None, "tile"),
            P(None, None, "tile"),
            P(None, "tile"),
            P("ens", None, "tile", None),
        ),
        out_specs=(
            P("ens", None, "tile", None),
            P("ens", "tile", None, None),
            P("ens", None, "tile", None),
            P(),
            P(),
            P(),
            P(),
            P(),
        ),
        check_vma=False,
    )
```

```python
import functools
import math

import jax
import jax.numpy as jnp
from jax import lax
from jax.experimental import pallas as pl
from jax.experimental.pallas import tpu as pltpu
from jax.sharding import PartitionSpec as P

SUBDIVISION = 4
KS = 3
LANES = 128
SLABS = 3
MESH = pl.DeviceIdType.MESH


def pack_plan(shapes):
    plan, at = [], 0
    for which, (rows, cols) in enumerate(shapes):
        for col in range(0, cols, LANES):
            plan.append((which, col, at, rows))
            at += rows
    return plan, at


def reduce_kernel(
    scale,
    ne,
    nt,
    rows,
    plan,
    used,
    up_ref,
    down_ref,
    force_ref,
    conv_ref,
    gain_ref,
    therm_ref,
    whole,
    therm_out,
    small,
    packed,
    from_core,
    halves,
    from_ens,
    part,
    from_z,
    therm_in,
    t_send,
    t_recv,
    a_send,
    a_recv,
    b_send,
    b_recv,
    c_send,
    c_recv,
    d_send,
    d_recv,
    e_send,
    e_recv,
    f_send,
    f_recv,
):
    nz = nt // 2
    block = nz * rows
    slab = 2 * ne * block
    ens = lax.axis_index("ens")
    tile = lax.axis_index("tile")
    z = tile // 2
    core = tile % 2
    other = 1 - core
    mate = {"tile": z * 2 + other}

    def send(src, dst, s_sem, r_sem, device):
        copy = pltpu.make_async_remote_copy(
            src_ref=src,
            dst_ref=dst,
            send_sem=s_sem,
            recv_sem=r_sem,
            device_id=device,
            device_id_type=MESH,
        )
        copy.start()
        return copy

    def at_block(s, h, e):
        return pl.ds(pl.multiple_of(s * slab + (h * ne + e) * block, 16), block)

    def at_chunk(where):
        return pl.ds(pl.multiple_of(where * rows, 16), rows)

    barrier = pltpu.get_barrier_semaphore()
    for o in range(1, nt):
        pl.semaphore_signal(
            barrier, inc=1, device_id={"tile": (tile + o) % nt}, device_id_type=MESH
        )
    for o in range(1, ne):
        pl.semaphore_signal(
            barrier, inc=1, device_id={"ens": (ens + o) % ne}, device_id_type=MESH
        )

    taps = len(conv_ref)
    small[...] = jnp.zeros_like(small)
    for tap in range(taps):
        small[tap : tap + 1, :] = conv_ref[tap][...]
    small[taps : taps + 1, :] = gain_ref[...]
    ins = (up_ref, down_ref, force_ref, small)
    if used < SLABS * slab:
        packed[used : SLABS * slab, :] = jnp.zeros((SLABS * slab - used, LANES), jnp.bfloat16)

    order = list(range(1, ne)) + [0]
    a_copies = [[] for _ in range(SLABS)]

    def send_slab(s):
        for o in order:
            e = (ens + o) % ne
            a_copies[s].append(
                send(
                    packed.at[at_block(s, other, e)],
                    from_core.at[s, o],
                    a_send.at[s, o],
                    a_recv.at[s, o],
                    mate,
                )
            )

    ready = 0
    for which, col, at, count in plan:
        packed[at : at + count, :] = ins[which][:, col : col + LANES].astype(jnp.bfloat16)
        while ready < SLABS and at + count >= min((ready + 1) * slab, used):
            if ready == 0:
                pl.semaphore_wait(barrier, nt - 1 + ne - 1)
            send_slab(ready)
            ready += 1

    t_copies = []
    for o in range(1, nt):
        to = (tile + o) % nt
        t_copies.append(
            send(
                therm_ref.at[to],
                therm_in.at[o],
                t_send.at[o],
                t_recv.at[o],
                {"tile": to},
            )
        )
    b_copies = [[] for _ in range(SLABS)]
    for s in range(SLABS):
        for o, copy in zip(order, a_copies[s]):
            e = (ens + o) % ne
            copy.wait_recv()
            halves[s, o] = (
                packed[at_block(s, core, e), :].astype(jnp.float32)
                + from_core[s, o].astype(jnp.float32)
            ).astype(jnp.bfloat16)
            if o:
                b_copies[s].append(
                    send(
                        halves.at[s, o],
                        from_ens.at[s, o],
                        b_send.at[s, o],
                        b_recv.at[s, o],
                        {"ens": e},
                    )
                )
    c_copies = [[] for _ in range(SLABS)]
    for s in range(SLABS):
        total = halves[s, 0].astype(jnp.float32)
        for o, copy in zip(range(1, ne), b_copies[s]):
            copy.wait_recv()
            total = total + from_ens[s, o].astype(jnp.float32)
        part[s] = total.astype(jnp.bfloat16)
        for o in range(1, nz):
            to = (z + o) % nz
            c_copies[s].append(
                send(
                    part.at[s, at_chunk(to)],
                    from_z.at[s, o],
                    c_send.at[s, o],
                    c_recv.at[s, o],
                    {"tile": to * 2 + core},
                )
            )
    d_copies = [[] for _ in range(SLABS)]
    for s in range(SLABS):
        mine = part[s, at_chunk(z), :].astype(jnp.float32)
        for o, copy in zip(range(1, nz), c_copies[s]):
            copy.wait_recv()
            mine = mine + from_z[s, o].astype(jnp.float32)
        spot = at_chunk(((s * 2 + core) * ne + ens) * nz + z)
        whole[spot, :] = (mine * scale).astype(jnp.bfloat16)
        for o in range(1, nz):
            to = (z + o) % nz
            d_copies[s].append(
                send(
                    whole.at[spot],
                    whole.at[spot],
                    d_send.at[s, o],
                    d_recv.at[s, o],
                    {"tile": to * 2 + core},
                )
            )
    e_copies = [[] for _ in range(SLABS)]
    f_copies = []
    for s in range(SLABS):
        for copy in d_copies[s]:
            copy.wait_recv()
        own = at_block(s, core, ens)
        for o in range(1, ne):
            e_copies[s].append(
                send(
                    whole.at[own],
                    whole.at[own],
                    e_send.at[s, o],
                    e_recv.at[s, o],
                    {"ens": (ens + o) % ne},
                )
            )
        f_copies.append(send(whole.at[own], whole.at[own], f_send.at[s, 0], f_recv.at[s, 0], mate))
    for s in range(SLABS):
        for o, copy in zip(range(1, ne), e_copies[s]):
            copy.wait_recv()
            theirs = at_block(s, core, (ens + ne - o) % ne)
            f_copies.append(
                send(whole.at[theirs], whole.at[theirs], f_send.at[s, o], f_recv.at[s, o], mate)
            )
    therm_out[tile] = therm_ref[tile]
    for o, copy in zip(range(1, nt), t_copies):
        copy.wait_recv()
        therm_out[(tile + nt - o) % nt] = therm_in[o]
    for copy in f_copies:
        copy.wait_recv()
    sent = t_copies + f_copies
    for group in (a_copies, b_copies, c_copies, d_copies, e_copies):
        for copies in group:
            sent = sent + copies
    for copy in sent:
        copy.wait_send()


def unpack_kernel(
    plan, whole, therm, up_out, down_out, force_out, conv_out, gain_out, therm_out, strip, sems
):
    outs = (up_out, down_out, force_out)
    copies = []
    for i, (which, col, at, count) in enumerate(plan):
        if which < len(outs):
            copies.append(
                pltpu.make_async_copy(
                    whole.at[at : at + count, :],
                    outs[which].at[:, col : col + LANES],
                    sems.at[i],
                )
            )
            copies[-1].start()
    taps = conv_out.shape[0]
    for which, col, at, count in plan:
        if which == len(outs):
            rows = whole[at : at + count, :].astype(jnp.float32)
            conv_out[:, col : col + LANES] = rows[:taps].astype(jnp.bfloat16)
            gain_out[col : col + LANES] = rows[taps].astype(jnp.bfloat16)
    tiles, columns, _ = therm.shape
    for t in range(tiles):
        strip[t * columns : (t + 1) * columns, :] = therm[t]
    therm_out[0] = strip[...].astype(jnp.bfloat16)
    for copy in copies:
        copy.wait()


def reduce_gradients(up, down, force, conv, gain, therm, scale):
    ne, nt = lax.axis_size("ens"), lax.axis_size("tile")
    nz = nt // 2
    taps, features = len(conv), conv[0].shape[1]
    small_rows = -(-(taps + 1) // 16) * 16
    plan, used = pack_plan([up.shape, down.shape, force.shape, (small_rows, features)])
    rows = -(-used // (SLABS * 2 * ne * nz * 16)) * 16
    block = nz * rows
    bf16 = jnp.bfloat16
    dma = pltpu.SemaphoreType.DMA
    vmem = pl.BlockSpec(memory_space=pltpu.VMEM)
    anywhere = pl.BlockSpec(memory_space=pl.ANY)
    tiles, columns, quantity = therm.shape
    whole, therm = pl.pallas_call(
        functools.partial(reduce_kernel, scale, ne, nt, rows, plan, used),
        out_shape=[
            jax.ShapeDtypeStruct((SLABS * 2 * ne * block, LANES), bf16),
            jax.ShapeDtypeStruct(therm.shape, therm.dtype),
        ],
        in_specs=[vmem] * 3 + [[vmem] * taps] + [vmem] * 2,
        out_specs=[vmem] * 2,
        scratch_shapes=[
            pltpu.VMEM((small_rows, features), jnp.float32),
            pltpu.VMEM((SLABS * 2 * ne * block, LANES), bf16),
            pltpu.VMEM((SLABS, ne, block, LANES), bf16),
            pltpu.VMEM((SLABS, ne, block, LANES), bf16),
            pltpu.VMEM((SLABS, ne, block, LANES), bf16),
            pltpu.VMEM((SLABS, block, LANES), bf16),
            pltpu.VMEM((SLABS, nz, rows, LANES), bf16),
            pltpu.VMEM(therm.shape, therm.dtype),
        ]
        + [dma((nt,)), dma((nt,))]
        + [dma((SLABS, ne)), dma((SLABS, ne))] * 2
        + [dma((SLABS, nz)), dma((SLABS, nz))] * 2
        + [dma((SLABS, ne)), dma((SLABS, ne))] * 2,
        compiler_params=pltpu.CompilerParams(collective_id=1, has_side_effects=True),
        name="reduce_gradients",
    )(up, down, force, conv, gain, therm)
    return pl.pallas_call(
        functools.partial(unpack_kernel, plan),
        out_shape=[
            jax.ShapeDtypeStruct(up.shape, bf16),
            jax.ShapeDtypeStruct(down.shape, bf16),
            jax.ShapeDtypeStruct(force.shape, bf16),
            jax.ShapeDtypeStruct((taps, features), bf16),
            jax.ShapeDtypeStruct((features,), bf16),
            jax.ShapeDtypeStruct((1, tiles * columns, quantity), bf16),
        ],
        in_specs=[vmem] * 2,
        out_specs=[anywhere] * 3 + [vmem] * 3,
        scratch_shapes=[
            pltpu.VMEM((tiles * columns, quantity), jnp.float32),
            dma((len(plan),)),
        ],
        name="unpack_gradients",
    )(whole, therm)


def mix_kernel(
    nt,
    cols,
    air_ref,
    exchange_ref,
    weights_ref,
    latent_ref,
    driver_ref,
    forcing_out,
    mixed_out,
    padded,
    flux,
    slabs,
    strip_in,
    strip,
    edges,
    halo,
    s_send,
    s_recv,
    h_send,
    h_recv,
):
    tile = lax.axis_index("tile")
    bf16, f32 = jnp.bfloat16, jnp.float32
    barrier = pltpu.get_barrier_semaphore()
    for o in range(1, nt):
        pl.semaphore_signal(
            barrier, inc=1, device_id={"tile": (tile + o) % nt}, device_id_type=MESH
        )
    flux[...] = (
        jnp.dot(air_ref[...], exchange_ref[...], preferred_element_type=f32)
        .astype(bf16)
        .astype(f32)
    )
    share = slabs.shape[1]
    for t in range(nt):
        slabs[t] = flux[t * share : (t + 1) * share, :]
    pl.semaphore_wait(barrier, nt - 1)
    copies = []
    for o in range(1, nt):
        to = (tile + o) % nt
        copies.append(
            pltpu.make_async_remote_copy(
                src_ref=slabs.at[to],
                dst_ref=strip_in.at[tile],
                send_sem=s_send.at[o],
                recv_sem=s_recv.at[o],
                device_id={"tile": to},
                device_id_type=MESH,
            )
        )
        copies[-1].start()
    strip_in[tile] = slabs[tile]
    weights = weights_ref[...]
    over_sites = (((0,), (0,)), ((), ()))
    total = lax.dot_general(
        weights,
        jnp.ones((weights.shape[0], strip.shape[1]), bf16),
        over_sites,
        preferred_element_type=f32,
    )
    for copy in copies:
        copy.wait_recv()
    for t in range(nt):
        strip[t * share : (t + 1) * share, :] = strip_in[t]
    weighted = lax.dot_general(
        weights, strip[...].astype(bf16), over_sites, preferred_element_type=f32
    )
    forcing = (weighted / total).astype(bf16)
    forcing_out[...] = forcing
    mixed = (
        latent_ref[...].astype(f32)
        + jnp.dot(forcing, driver_ref[...], preferred_element_type=f32)
    ).astype(bf16)
    cube = mixed.astype(f32).reshape(edges.shape[1], cols, mixed.shape[1])
    edges[0] = cube[:, cols - 1 : cols, :]
    edges[1] = cube[:, 0:1, :]
    hops = ((0, (tile + 1) % nt), (1, (tile + nt - 1) % nt))
    halos = []
    for side, to in hops:
        halos.append(
            pltpu.make_async_remote_copy(
                src_ref=edges.at[side],
                dst_ref=halo.at[side],
                send_sem=h_send.at[side],
                recv_sem=h_recv.at[side],
                device_id={"tile": to},
                device_id_type=MESH,
            )
        )
        halos[-1].start()
    mixed_out[...] = mixed
    rows = edges.shape[1]
    padded[0] = jnp.zeros_like(padded[0])
    padded[rows + 1] = jnp.zeros_like(padded[0])
    padded[1 : rows + 1, 1 : cols + 1, :] = cube
    for copy in halos:
        copy.wait_recv()
    padded[1 : rows + 1, 0:1, :] = halo[0]
    padded[1 : rows + 1, cols + 1 : cols + 2, :] = halo[1]
    for copy in copies + halos:
        copy.wait_send()


def mix_states(band, exchange, sites, margin, latent, driver):
    nt = lax.axis_size("tile")
    rows, cols, features = latent.shape
    quantity = exchange.shape[1]
    places = band.shape[0]
    cells = rows * cols
    both = (margin * places + sites).reshape(sites.shape[0], 1, cells)
    flat_sites, flat_margin = both % places, both // places
    names = lax.broadcasted_iota(jnp.int32, (1, places, 1), 1)
    weights = jnp.sum(jnp.where(flat_sites == names, flat_margin, 0), axis=0)
    bf16, f32 = jnp.bfloat16, jnp.float32
    dma = pltpu.SemaphoreType.DMA
    vmem = pl.BlockSpec(memory_space=pltpu.VMEM)
    return pl.pallas_call(
        functools.partial(mix_kernel, nt, cols),
        out_shape=[
            jax.ShapeDtypeStruct((cells, quantity), bf16),
            jax.ShapeDtypeStruct((cells, features), bf16),
            jax.ShapeDtypeStruct((rows + 2, cols + 2, features), f32),
        ],
        in_specs=[vmem] * 5,
        out_specs=[vmem] * 3,
        scratch_shapes=[
            pltpu.VMEM((places, quantity), f32),
            pltpu.VMEM((nt, places // nt, quantity), f32),
            pltpu.VMEM((nt, places // nt, quantity), f32),
            pltpu.VMEM((places, quantity), f32),
            pltpu.VMEM((2, rows, 1, features), f32),
            pltpu.VMEM((2, rows, 1, features), f32),
            dma((nt,)),
            dma((nt,)),
            dma((2,)),
            dma((2,)),
        ],
        compiler_params=pltpu.CompilerParams(collective_id=2, has_side_effects=True),
        name="mix_states",
    )(band, exchange, weights.astype(bf16), latent.reshape(cells, features), driver)


def extended(cells, sides, width):
    for axis, dim in sides:
        count = lax.axis_size(axis)
        head = lax.slice_in_dim(cells, 0, width, axis=dim)
        tail = lax.slice_in_dim(cells, cells.shape[dim] - width, cells.shape[dim], axis=dim)
        cells = jnp.concatenate(
            [
                lax.ppermute(tail, axis, [(i, (i + 1) % count) for i in range(count)]),
                cells,
                lax.ppermute(head, axis, [((i + 1) % count, i) for i in range(count)]),
            ],
            axis=dim,
        )
    return cells


def layer_norm(values, gain):
    centred = values - jnp.mean(values, axis=-1, keepdims=True)
    spread = jnp.mean(centred * centred, axis=-1, keepdims=True)
    return centred * lax.rsqrt(spread + 1e-06) * gain


def marine_update_kernel(
    marine_present_latent,
    marine_driver_input,
    latent_adjoint,
    water_indicator_real,
    driver_projection_matrix,
    spatial_kernel_taps,
    layernorm_multiplier,
    pointwise_widen_matrix,
    pointwise_shrink_matrix,
    thermal_projection_matrix,
    haloed_derivative,
):
    horizontal_sum_result, vertical_sum_result, feature_dimension = marine_present_latent.shape
    reach = KS // 2
    forcing_flat, mixed, padded = marine_driver_input
    mixed = mixed.reshape(horizontal_sum_result, vertical_sum_result, feature_dimension)
    conv_out = jnp.zeros(
        (horizontal_sum_result, vertical_sum_result, feature_dimension), jnp.float32
    )
    for row_off in range(KS):
        for col_off in range(KS):
            conv_out = (
                conv_out
                + spatial_kernel_taps[row_off * KS + col_off]
                * padded[
                    row_off : row_off + horizontal_sum_result,
                    col_off : col_off + vertical_sum_result,
                ]
            )
    normed_f, pull_norm = jax.vjp(
        layer_norm, conv_out.reshape(-1, feature_dimension), layernorm_multiplier
    )
    normed = normed_f.astype(jnp.bfloat16)
    hidden_pre = jnp.dot(normed, pointwise_widen_matrix, preferred_element_type=jnp.float32)
    hidden_f, pull_gelu = jax.vjp(jax.nn.gelu, hidden_pre)
    hidden = hidden_f.astype(jnp.bfloat16)
    mlp_out = jnp.dot(hidden, pointwise_shrink_matrix, preferred_element_type=jnp.float32)
    sea_column = water_indicator_real.reshape(-1, 1)
    marine_successor_latent = (
        sea_column * (mixed.reshape(-1, feature_dimension).astype(jnp.float32) + mlp_out)
    ).astype(jnp.bfloat16)
    thermal_highres_field = jnp.dot(
        marine_successor_latent, thermal_projection_matrix, preferred_element_type=jnp.float32
    )
    thermal_highres_field = thermal_highres_field.reshape(
        horizontal_sum_result // SUBDIVISION,
        SUBDIVISION,
        vertical_sum_result // SUBDIVISION,
        SUBDIVISION,
        thermal_highres_field.shape[-1],
    )
    marine_site_number = jnp.sum(
        water_indicator_real.reshape(
            horizontal_sum_result // SUBDIVISION,
            SUBDIVISION,
            vertical_sum_result // SUBDIVISION,
            SUBDIVISION,
        ),
        axis=(1, 3),
    )
    thermal_lowres_field = (
        jnp.sum(thermal_highres_field, axis=(1, 3))
        / jnp.maximum(marine_site_number, 1.0)[..., None]
    ).astype(jnp.bfloat16)
    masked_cot = (
        sea_column * latent_adjoint.reshape(-1, feature_dimension).astype(jnp.float32)
    ).astype(jnp.bfloat16)
    grad_down = jnp.dot(hidden.T, masked_cot, preferred_element_type=jnp.float32)
    hidden_cot = jnp.dot(masked_cot, pointwise_shrink_matrix.T, preferred_element_type=jnp.float32)
    pre_cot = pull_gelu(hidden_cot)[0].astype(jnp.bfloat16)
    grad_up = jnp.dot(normed.T, pre_cot, preferred_element_type=jnp.float32)
    normed_cot = jnp.dot(pre_cot, pointwise_widen_matrix.T, preferred_element_type=jnp.float32)
    conv_cot, grad_gain = pull_norm(normed_cot)
    conv_cot = conv_cot.reshape(horizontal_sum_result, vertical_sum_result, feature_dimension)
    tap_grads = []
    for row_off in range(KS):
        for col_off in range(KS):
            tap_grads.append(
                jnp.sum(
                    conv_cot
                    * padded[
                        row_off : row_off + horizontal_sum_result,
                        col_off : col_off + vertical_sum_result,
                    ],
                    axis=(0, 1),
                )
            )
    grad_padded = jnp.pad(haloed_derivative(conv_cot), ((reach, reach), (0, 0), (0, 0)))
    back = masked_cot.astype(jnp.float32).reshape(
        horizontal_sum_result, vertical_sum_result, feature_dimension
    )
    for row_off in range(KS):
        for col_off in range(KS):
            row_from = KS - 1 - row_off
            col_from = KS - 1 - col_off
            back = (
                back
                + spatial_kernel_taps[row_off * KS + col_off]
                * grad_padded[
                    row_from : row_from + horizontal_sum_result,
                    col_from : col_from + vertical_sum_result,
                ]
            )
    marine_latent_adjoint = back.astype(jnp.bfloat16)
    grad_force = jnp.dot(
        forcing_flat.T,
        marine_latent_adjoint.reshape(-1, feature_dimension),
        preferred_element_type=jnp.float32,
    )
    derivative_sequence = (grad_force, [values.reshape(1, -1) for values in tap_grads], grad_gain, grad_up, grad_down)
    return (
        marine_successor_latent.reshape(
            horizontal_sum_result, vertical_sum_result, feature_dimension
        ),
        thermal_lowres_field,
        marine_latent_adjoint,
        derivative_sequence,
    )


def pad_grad_cols(values):
    return extended(values, (("tile", 1),), KS // 2)


def body(
    air_latent_array,
    air_exchange_projection,
    marine_latent_array,
    driver_projection_matrix,
    spatial_kernel_taps,
    layernorm_multiplier,
    pointwise_widen_matrix,
    pointwise_shrink_matrix,
    thermal_projection_matrix,
    intersecting_air_sites,
    margin_multiplier,
    terrain_water_indicator,
    marine_successor_adjoint,
):
    band = air_latent_array[0]
    band_rows, band_cols, atmos_width = band.shape
    marine_driver_input = mix_states(
        band.reshape(-1, atmos_width),
        air_exchange_projection,
        intersecting_air_sites,
        margin_multiplier,
        marine_latent_array[0],
        driver_projection_matrix,
    )
    water_indicator_real = terrain_water_indicator.astype(jnp.float32)
    marine_successor_latent, thermal_lowres_field, marine_latent_adjoint, derivative_sequence = (
        marine_update_kernel(
            marine_latent_array[0],
            marine_driver_input,
            marine_successor_adjoint[0],
            water_indicator_real,
            driver_projection_matrix,
            spatial_kernel_taps,
            layernorm_multiplier,
            pointwise_widen_matrix,
            pointwise_shrink_matrix,
            thermal_projection_matrix,
            pad_grad_cols,
        )
    )
    cell_total = (
        lax.axis_size("ens")
        * lax.axis_size("tile")
        * marine_successor_latent.shape[0]
        * marine_successor_latent.shape[1]
    )
    grad_scale = 1.0 / math.sqrt(cell_total)
    grad_force, grad_conv, grad_gain, grad_up, grad_down = derivative_sequence
    up, down, force, conv, gain, thermal_strip_slice = reduce_gradients(
        grad_up,
        grad_down,
        grad_force,
        grad_conv,
        grad_gain.reshape(1, -1),
        thermal_lowres_field.astype(jnp.float32),
        grad_scale,
    )
    return (
        marine_successor_latent[None],
        thermal_strip_slice[None],
        marine_latent_adjoint[None],
        force,
        conv,
        gain,
        up,
        down,
    )


def solution(mesh):
    return jax.shard_map(
        body,
        mesh=mesh,
        in_specs=(
            P("ens", "tile", None, None),
            P(),
            P("ens", None, "tile", None),
            P(),
            P(),
            P(),
            P(),
            P(),
            P(),
            P(None, None, "tile"),
            P(None, None, "tile"),
            P(None, "tile"),
            P("ens", None, "tile", None),
        ),
        out_specs=(
            P("ens", None, "tile", None),
            P("ens", "tile", None, None),
            P("ens", None, "tile", None),
            P(),
            P(),
            P(),
            P(),
            P(),
        ),
        check_vma=False,
    )
```
